32 devices in a mesh: groups: 2 (over x), vid: 8 (over z, y), tok: 2 (over core).
Axes of the slice: x: 2, y: 2, z: 4, core: 2. Of those that a mesh axis runs over, the one named last changes fastest.
Arguments:
- captions: bfloat16 [16, 128, 32, 128], P(('groups', 'vid')), parts along dimension 0, may hold values from -8 to 8
- caption_lengths: int32 [16, 128], P(('groups', 'vid')), parts along dimension 0, may hold values from 1 to 32
- video_bank: bfloat16 [192, 256, 128], P(('groups', 'vid'), 'tok'), parts along dimension 0, may hold values from -1.5 to 1.5
- owner_order: int32 [6], P('groups'), parts along dimension 0, may hold values from 0 to 7, as said below
Outputs:
- scores: float32 [192, 384], P(('groups', 'vid')), parts along dimension 0
The draws below stay inside these ranges and needn't reach their ends.
There are 2 independent parts, one for each index of `groups`. The reference program is written for one: setup_inputs(seed, part) draws one part's arguments, and reference() takes and returns one part's arrays. A program takes and returns all parts, laid end to end along the dimension named above; each array names one. Nothing has to cross between parts.
Inputs may be any that keep to these rules, and one draw needn't show every extreme that they name: `caption_lengths`: token slot j of a caption is real when j is less than its count. `owner_order`: 3 different block indices.
All inputs are finite; a program needn't handle non-finite values.
Results may differ from the reference program's by a relative error of at most 0.0003.
Values may be sent and summed in bfloat16 or wider, within the bound.
No kernel may reach another device: no remote copies, remote signals or barrier semaphores. Data moves between devices by JAX's collectives and lax.ppermute only.
A program may use at most 64 MiB of HBM per device.

```python
import jax
import jax.numpy as jnp
from jax import lax

D = 128
LQ = 32
VTOK = 256
CAPB = 128
ROUNDS = 3
VIDEOS = 96
CAP_OWNERS = 8


def draw_captions(key, part):
    shape_full = (CAP_OWNERS, CAPB, LQ, D)
    values_out = jnp.clip(jax.random.normal(jax.random.fold_in(key, 12), shape_full, jnp.float32), -6.0, 6.0)
    return jnp.clip(values_out, -8.0, 8.0).astype(jnp.bfloat16)


def draw_video_bank(key, part):
    shape_full = (VIDEOS, VTOK, D)
    spread = 0.6 * D ** (-0.5)
    values_out = jnp.clip(jax.random.normal(jax.random.fold_in(key, 23), shape_full, jnp.float32) * spread, -6.0 * spread, 6.0 * spread)
    return jnp.clip(values_out, -1.5, 1.5).astype(jnp.bfloat16)


def draw_owner_order(key, part):
    shuffled = jax.random.permutation(jax.random.fold_in(key, 31), CAP_OWNERS)
    return shuffled[:ROUNDS].astype(jnp.int32)


def plant(result, key, low, high):
    extent = result.shape
    place = [jax.random.randint(jax.random.fold_in(key, axis), (), 0, extent[axis]) for axis in range(len(extent))]
    result = result.at[tuple(place)].set(low)
    longest = extent.index(max(extent))
    place[longest] = (place[longest] + 1) % extent[longest]
    return result.at[tuple(place)].set(high)


def setup_inputs(seed: int = 0, part: int = 0) -> dict:
    seeds = jax.random.split(jax.random.key(seed), 5)
    own_keys = jax.random.split(jax.random.fold_in(seeds[4], part), 5)
    captions = draw_captions(jax.random.fold_in(jax.random.fold_in(seeds[4], part), 71), part)
    caption_lengths = plant(jax.random.randint(own_keys[1], (CAP_OWNERS, CAPB), 1, LQ + 1), jax.random.fold_in(own_keys[1], 1), 1, LQ).astype(jnp.int32)
    video_bank = draw_video_bank(jax.random.fold_in(jax.random.fold_in(seeds[4], part), 71), part)
    owner_order = draw_owner_order(jax.random.fold_in(jax.random.fold_in(seeds[4], part), 71), part)
    return {"captions": captions, "caption_lengths": caption_lengths, "video_bank": video_bank, "owner_order": owner_order}


sharpness_factor = 5.0


def reference(captions, caption_lengths, video_bank, owner_order):
    bank_full = video_bank.astype(jnp.float32)
    results = []
    for round_index in range(ROUNDS):
        caption_rows = captions[owner_order[round_index]].astype(jnp.float32)
        counts = caption_lengths[owner_order[round_index]]
        query_rows = caption_rows.reshape(CAPB * LQ, D)

        def per_video(footage_key_matrix):
            raw_similarity = jnp.dot(query_rows, footage_key_matrix.T, precision=lax.Precision.HIGHEST) * sharpness_factor
            row_peak = jnp.max(raw_similarity, axis=1)
            row_accumulated = jnp.sum(jnp.exp(raw_similarity - row_peak[:, None]), axis=1)
            return (row_peak + jnp.log(row_accumulated)) / sharpness_factor

        smoothed_scores = lax.map(per_video, bank_full).reshape(VIDEOS, CAPB, LQ)
        slots = jnp.arange(LQ, dtype=jnp.int32)
        lengths_float = counts.astype(jnp.float32)
        weights = (slots[None, :] < counts[:, None]).astype(jnp.float32) / lengths_float[:, None]
        results.append(jnp.einsum("vcj,cj->vc", smoothed_scores, weights, precision=lax.Precision.HIGHEST))
    return jnp.concatenate(results, axis=1)
```

```python
import jax
import jax.numpy as jnp
from jax import lax
from jax.experimental import pallas as pl
from jax.experimental.pallas import tpu as pltpu
from jax.sharding import PartitionSpec as P

SHARPNESS = 5.0
LOG2E = 1.4426950408889634
LN2 = 0.6931471805599453
COUNT_ROWS = 8
PAIR = 2


def score_kernel(slots, caps, q_ref, own_ref, tok_ref, pair_ref, both_ref, out_ref, top_ref, sum_ref):
    videos = own_ref.shape[0]
    rows = caps * slots
    query = q_ref[0, :rows, :]
    scale = jnp.float32(SHARPNESS * LOG2E)

    def one(v, at, a_ref, b_ref):
        parts = []
        for ref in (a_ref, b_ref):
            raw = lax.dot_general(
                ref[v], query, (((1,), (1,)), ((), ())), preferred_element_type=jnp.float32
            )
            parts.append((raw * scale).reshape(raw.shape[0] // 8, 8, rows))
        top = jnp.maximum(jnp.max(parts[0], axis=0), jnp.max(parts[1], axis=0))
        total = jnp.sum(jnp.exp2(parts[0] - top[None]), axis=0)
        total = total + jnp.sum(jnp.exp2(parts[1] - top[None]), axis=0)
        top_ref[at] = top
        sum_ref[at] = total

    def step(v, carry):
        one(v, v, own_ref, tok_ref)
        one(v, v + videos, pair_ref, both_ref)
        return carry

    lax.fori_loop(0, videos, step, 0)

    tops = top_ref[...]
    peak = jnp.max(tops, axis=1)
    total = jnp.sum(sum_ref[...] * jnp.exp2(tops - peak[:, None, :]), axis=1)
    soft = (peak + jnp.log2(total)) * jnp.float32(LN2 / SHARPNESS)

    counts = q_ref[0, rows : rows + 8, :].astype(jnp.float32)[0:1, :]
    row = lax.broadcasted_iota(jnp.int32, (rows, 128), 0)
    cap = lax.broadcasted_iota(jnp.int32, (rows, 128), 1)
    first = cap * slots
    last = first + counts.astype(jnp.int32)
    member = ((row >= first) & (row < last) & (cap < caps)).astype(jnp.float32)
    picked = lax.dot_general(
        soft, member, (((1,), (0,)), ((), ())),
        precision=lax.Precision.HIGHEST, preferred_element_type=jnp.float32,
    )
    out_ref[0] = picked / jnp.maximum(counts, 1.0)


def per_device(captions, caption_lengths, video_bank, owner_order):
    n_vid, n_tok = lax.axis_size("vid"), lax.axis_size("tok")
    capb, slots, width = captions.shape[1:]
    videos = video_bank.shape[0]
    rounds = owner_order.shape[0]
    line = n_vid // PAIR
    caps = capb // (n_vid * n_tok)
    rows = caps * slots
    tok = lax.axis_index("tok")
    side = lax.axis_index("vid") % PAIR

    swap_tok = [(0, 1), (1, 0)]
    swap_pair = [(i, i ^ 1) for i in range(n_vid)]
    tok_bank = lax.ppermute(video_bank, "tok", swap_tok)
    pair_bank = lax.ppermute(video_bank, "vid", swap_pair)
    both_bank = lax.ppermute(pair_bank, "tok", swap_tok)

    split = captions.reshape(PAIR, n_tok, line, rows, width)
    mine = lax.dynamic_index_in_dim(split, tok, 1, keepdims=False)
    counts = caption_lengths.reshape(PAIR, n_tok, line, 1, caps)
    counts = lax.dynamic_index_in_dim(counts, tok, 1, keepdims=False).astype(captions.dtype)
    counts = jnp.pad(counts, ((0, 0), (0, 0), (0, COUNT_ROWS - 1), (0, width - caps)))
    pieces = jnp.concatenate([mine, counts], axis=2)
    pieces = pieces.transpose(1, 0, 2, 3).reshape(n_vid, rows + COUNT_ROWS, width)
    shares = lax.all_to_all(pieces, "vid", 0, 0, tiled=True)
    wanted = jnp.stack(
        [lax.dynamic_index_in_dim(shares, owner_order[r], 0, keepdims=False) for r in range(rounds)]
    )
    lines = [[k * PAIR + s for k in range(line)] for s in range(PAIR)]
    query = lax.all_gather(wanted, "vid", axis=0, tiled=True, axis_index_groups=lines)

    whole = lambda shape: pl.BlockSpec(shape, lambda i: (0,) * len(shape))
    tiles = line * rounds
    scores = pl.pallas_call(
        lambda *refs: score_kernel(slots, caps, *refs),
        grid=(tiles,),
        in_specs=[pl.BlockSpec((1, rows + COUNT_ROWS, width), lambda i: (i, 0, 0))]
        + [whole(video_bank.shape)] * 4,
        out_specs=pl.BlockSpec((1, 2 * videos, 128), lambda i: (i, 0, 0)),
        out_shape=jax.ShapeDtypeStruct((tiles, 2 * videos, 128), jnp.float32),
        scratch_shapes=[pltpu.VMEM((2 * videos, 8, rows), jnp.float32)] * 2,
        name="soft_scores",
    )(query, video_bank, tok_bank, pair_bank, both_bank)

    scores = scores[:, :, :caps].reshape(line, rounds, PAIR, videos, caps)
    scores = scores.transpose(2, 3, 1, 0, 4).reshape(PAIR, videos, rounds, line * caps)
    theirs = lax.ppermute(scores[1], "vid", swap_pair)
    halves = jnp.stack([scores[0], theirs])
    halves = jnp.where(side == 0, halves, halves[::-1])
    other = lax.ppermute(halves, "tok", swap_tok)
    quarters = jnp.stack([jnp.where(tok == 0, halves, other), jnp.where(tok == 0, other, halves)])
    return quarters.transpose(2, 3, 1, 0, 4).reshape(videos, rounds * capb)


def solution(mesh):
    return jax.shard_map(
        per_device,
        mesh=mesh,
        in_specs=(
            P(("groups", "vid"), None, None, None),
            P(("groups", "vid"), None),
            P(("groups", "vid"), "tok", None),
            P("groups"),
        ),
        out_specs=P(("groups", "vid"), None),
        check_vma=False,
    )
```

```python
import jax
import jax.numpy as jnp
from jax import lax
from jax.experimental import pallas as pl
from jax.experimental.pallas import tpu as pltpu
from jax.sharding import PartitionSpec as P

SHARPNESS = 5.0
LOG2E = 1.4426950408889634
LN2 = 0.6931471805599453
COUNT_ROWS = 8
PAIR = 2
TILE = 256
LANES = 128
JOBS = 2
VMEM_BYTES = 24 << 20
F32 = jnp.float32
BF16 = jnp.bfloat16


def dot(a, b, dims):
    return lax.dot_general(a, b, (dims, ((), ())), preferred_element_type=F32)


def score_kernel(slots, caps, meta_ref, lanes_ref, q_hbm, own_ref, tok_ref, pair_ref, both_ref,
                 out_ref, q_ref, bank_ref, rows_ref, soft_ref, a_ref, b_ref, sems):
    line, rounds = q_ref.shape[:2]
    quarters = LANES // (line * caps)
    videos, half = own_ref.shape[:2]
    tokens = 2 * half
    fetch_q = pltpu.make_async_copy(q_hbm, q_ref, sems.at[0])
    fetch_q.start()
    banks = []
    for k, src in enumerate((own_ref, tok_ref, pair_ref, both_ref)):
        dst = bank_ref.at[pl.ds(k // 2 * videos, videos), pl.ds(k % 2 * half, half), :]
        banks.append(pltpu.make_async_copy(src, dst, sems.at[1 + k]))
        banks[-1].start()
    fetch_q.wait()
    total_rows, quarter = meta_ref[2 * rounds, 0], meta_ref[2 * rounds, 1]

    def pack(i, carry):
        r, g = i // line, i % line
        piece = q_ref[g, r].astype(F32)
        for c in range(caps):
            start = meta_ref[r, (g * quarters + quarter) * caps + c]
            rows_ref[pl.ds(start, slots), :] = piece[c * slots : (c + 1) * slots]
        return carry

    lax.fori_loop(0, rounds * line, pack, 0)
    for copy in banks:
        copy.wait()
    out_ref[...] = jnp.zeros_like(out_ref)
    scale = F32(SHARPNESS * LOG2E)
    per = 2 * videos // JOBS
    jobs = [k * per for k in range(JOBS)]
    bufs = (a_ref, b_ref)

    def products(dst, first, w):
        bank = bank_ref[first : first + per].reshape(per * tokens, bank_ref.shape[2])
        dst[...] = dot(jnp.concatenate([bank, bank], axis=1), w, ((1,), (1,)))

    def unit(src, v, col):
        x = src[v * tokens : (v + 1) * tokens, col : col + LANES].reshape(tokens // 8, 8, LANES)
        top = jnp.max(x, axis=0)
        total = jnp.sum(jnp.exp2(x - top[None]), axis=0)
        peak = jnp.max(top, axis=0, keepdims=True)
        return peak, jnp.sum(total * jnp.exp2(top - peak), axis=0, keepdims=True)

    def weights(i):
        q = rows_ref[pl.ds(pl.multiple_of(i * TILE, TILE), TILE), :] * scale
        high = q.astype(BF16)
        return jnp.concatenate([high, (q - high.astype(F32)).astype(BF16)], axis=1)

    def collect(i):
        soft = (soft_ref[0] + jnp.log2(soft_ref[1])) * F32(LN2 / SHARPNESS)
        col = i * TILE + lax.broadcasted_iota(jnp.int32, soft.shape, 1)
        soft = jnp.where((col >= 0) & (col < total_rows), soft, 0.0)
        parts = []
        for _ in range(3):
            parts.append(soft.astype(BF16))
            soft = soft - parts[-1].astype(F32)
        parts = jnp.concatenate(parts, axis=0)
        row = i * TILE + lax.broadcasted_iota(jnp.int32, (TILE, LANES), 0)
        n = 2 * videos
        for r in range(rounds):
            first, count = lanes_ref[r : r + 1, :], lanes_ref[rounds + r : rounds + r + 1, :]
            member = jnp.where((row >= first) & (row < first + count), F32(1), F32(0))
            got = dot(parts, member.astype(BF16), ((1,), (0,)))
            out_ref[:, r * LANES : (r + 1) * LANES] += got[:n] + got[n : 2 * n] + got[2 * n :]

    def tile(i, carry):
        w = weights(i)
        collect(i - 1)
        for j, first in enumerate(jobs):
            after = (jobs[j + 1], w) if j + 1 < len(jobs) else (jobs[0], weights(i + 1))
            products(bufs[(j + 1) % 2], *after)
            for v in range(per):
                for col in range(0, TILE, LANES):
                    peak, total = unit(bufs[j % 2], v, col)
                    at = first + v
                    soft_ref[0, at : at + 1, col : col + LANES] = peak
                    soft_ref[1, at : at + 1, col : col + LANES] = total
        return carry

    products(bufs[0], jobs[0], weights(0))
    tiles = (total_rows + TILE - 1) // TILE
    lax.fori_loop(0, tiles, tile, 0)
    collect(tiles - 1)
    for r in range(rounds):
        count = jnp.maximum(lanes_ref[rounds + r : rounds + r + 1, :], 1).astype(F32)
        out_ref[:, r * LANES : (r + 1) * LANES] = out_ref[:, r * LANES : (r + 1) * LANES] / count


def pair_scores(slots, caps, meta, query, banks):
    line, rounds, rows, width = query.shape
    videos, half = banks[0].shape[:2]
    n_rows = -(-(rounds * line * rows) // TILE) * TILE + TILE + slots
    vmem = pl.BlockSpec(memory_space=pltpu.VMEM)
    anywhere = pl.BlockSpec(memory_space=pl.ANY)
    return pl.pallas_call(
        lambda *refs: score_kernel(slots, caps, *refs),
        in_specs=[pl.BlockSpec(memory_space=pltpu.SMEM), vmem] + [anywhere] * 5,
        out_specs=vmem,
        out_shape=jax.ShapeDtypeStruct((2 * videos, rounds * LANES), F32),
        scratch_shapes=[
            pltpu.VMEM(query.shape, query.dtype),
            pltpu.VMEM((2 * videos, 2 * half, width), banks[0].dtype),
            pltpu.VMEM((n_rows, width), F32),
            pltpu.VMEM((2, 2 * videos, TILE), F32),
            pltpu.VMEM((2 * videos // JOBS * 2 * half, TILE), F32),
            pltpu.VMEM((2 * videos // JOBS * 2 * half, TILE), F32),
            pltpu.SemaphoreType.DMA((5,)),
        ],
        compiler_params=pltpu.CompilerParams(vmem_limit_bytes=VMEM_BYTES),
        name="soft_scores",
    )(meta, meta, query, *banks)


def per_device(captions, caption_lengths, video_bank, owner_order):
    n_vid, n_tok = lax.axis_size("vid"), lax.axis_size("tok")
    capb, slots, width = captions.shape[1:]
    rounds = owner_order.shape[0]
    videos = video_bank.shape[0]
    line = n_vid // PAIR
    caps = capb // (n_vid * n_tok)
    rows = caps * slots
    tok = lax.axis_index("tok")
    quarter = lax.axis_index("vid") % PAIR * n_tok + tok
    swap_tok = [(0, 1), (1, 0)]
    swap_pair = [(i, i ^ 1) for i in range(n_vid)]

    tok_bank = lax.ppermute(video_bank, "tok", swap_tok)
    pair_bank = lax.ppermute(video_bank, "vid", swap_pair)
    both_bank = lax.ppermute(tok_bank, "vid", swap_pair)

    mine = lax.dynamic_index_in_dim(
        captions.reshape(n_vid, n_tok, rows, width), tok, 1, keepdims=False
    )
    counts = jnp.pad(caption_lengths.astype(captions.dtype), ((0, COUNT_ROWS - 1), (0, width - capb)))
    counts = jnp.broadcast_to(counts, (n_vid, COUNT_ROWS, width))
    pieces = jnp.concatenate([mine, counts], axis=1)
    shares = lax.all_to_all(pieces, "vid", 0, 0, tiled=True)
    owners = [owner_order[r] for r in range(rounds)]
    wanted = jnp.concatenate(
        [lax.dynamic_index_in_dim(shares, o, 0, keepdims=False)[:rows] for o in owners]
    )
    lines = [[k * PAIR + s for k in range(line)] for s in range(PAIR)]
    query = lax.all_gather(wanted, "vid", axis=0, axis_index_groups=lines)
    query = query.reshape(line, rounds, rows, width)

    counts = jnp.concatenate(
        [lax.dynamic_slice(shares, (o, rows, 0), (1, 1, capb)).reshape(1, capb) for o in owners]
    ).astype(jnp.int32)
    lane = jnp.arange(capb, dtype=jnp.int32)
    counts = jnp.where(lane // caps % (PAIR * n_tok) == quarter, counts, 0)
    flat = counts.reshape(rounds * capb)
    place = jnp.arange(rounds * capb, dtype=jnp.int32)
    starts = jnp.sum(jnp.where(place[None, :] < place[:, None], flat[None, :], 0), axis=1)
    tail = jnp.where(lane == 0, jnp.sum(flat), jnp.where(lane == 1, quarter, 0))
    meta = jnp.concatenate([starts.reshape(rounds, capb), counts, tail[None]])
    meta = jnp.pad(meta, ((0, -meta.shape[0] % 8), (0, 0)))

    scores = pair_scores(slots, caps, meta, query, (video_bank, tok_bank, pair_bank, both_bank))
    scores = scores[:videos] + lax.ppermute(scores[videos:], "vid", swap_pair)
    return scores + lax.ppermute(scores, "tok", swap_tok)


def solution(mesh):
    return jax.shard_map(
        per_device,
        mesh=mesh,
        in_specs=(
            P(("groups", "vid"), None, None, None),
            P(("groups", "vid"), None),
            P(("groups", "vid"), "tok", None),
            P("groups"),
        ),
        out_specs=P(("groups", "vid"), None),
        check_vma=False,
    )
```

```python
import jax
import jax.numpy as jnp
from jax import lax
from jax.experimental import pallas as pl
from jax.experimental.pallas import tpu as pltpu
from jax.sharding import PartitionSpec as P

SHARPNESS = 5.0
LOG2E = 1.4426950408889634
LN2 = 0.6931471805599453
COUNT_ROWS = 8
PAIR = 2
TILE = 256
LANES = 128
JOBS = 2
VMEM_BYTES = 24 << 20
F32 = jnp.float32
BF16 = jnp.bfloat16


def dot(a, b, dims):
    return lax.dot_general(a, b, (dims, ((), ())), preferred_element_type=F32)


def score_kernel(slots, caps, meta_ref, lanes_ref, q_hbm, own_ref, tok_ref, pair_ref, both_ref,
                 near_ref, far_ref, q_ref, bank_ref, out_ref, rows_ref,
                 soft_ref, a_ref, b_ref, sems):
    line, rounds = q_ref.shape[:2]
    quarters = LANES // (line * caps)
    videos, half = own_ref.shape[:2]
    tokens = 2 * half
    fetch_q = pltpu.make_async_copy(q_hbm, q_ref, sems.at[0])
    fetch_q.start()
    banks = []
    for k, src in enumerate((own_ref, tok_ref, pair_ref, both_ref)):
        dst = bank_ref.at[pl.ds(k // 2 * videos, videos), pl.ds(k % 2 * half, half), :]
        banks.append(pltpu.make_async_copy(src, dst, sems.at[1 + k]))
        banks[-1].start()
    fetch_q.wait()
    total_rows, quarter = meta_ref[2 * rounds, 0], meta_ref[2 * rounds, 1]

    def pack(i, carry):
        r, g = i // line, i % line
        piece = q_ref[g, r].astype(F32)
        for c in range(caps):
            start = meta_ref[r, (g * quarters + quarter) * caps + c]
            rows_ref[pl.ds(start, slots), :] = piece[c * slots : (c + 1) * slots]
        return carry

    lax.fori_loop(0, rounds * line, pack, 0)
    for copy in banks:
        copy.wait()
    out_ref[...] = jnp.zeros_like(out_ref)
    scale = F32(SHARPNESS * LOG2E)
    per = 2 * videos // JOBS
    jobs = [k * per for k in range(JOBS)]
    bufs = (a_ref, b_ref)

    def products(dst, first, w):
        bank = bank_ref[first : first + per].reshape(per * tokens, bank_ref.shape[2])
        dst[...] = dot(jnp.concatenate([bank, bank], axis=1), w, ((1,), (1,)))

    def unit(src, v, col):
        x = src[v * tokens : (v + 1) * tokens, col : col + LANES].reshape(tokens // 8, 8, LANES)
        top = jnp.max(x, axis=0)
        total = jnp.sum(jnp.exp2(x - top[None]), axis=0)
        peak = jnp.max(top, axis=0, keepdims=True)
        return peak, jnp.sum(total * jnp.exp2(top - peak), axis=0, keepdims=True)

    def weights(i):
        q = rows_ref[pl.ds(pl.multiple_of(i * TILE, TILE), TILE), :] * scale
        high = q.astype(BF16)
        return jnp.concatenate([high, (q - high.astype(F32)).astype(BF16)], axis=1)

    def collect(i):
        soft = (soft_ref[0] + jnp.log2(soft_ref[1])) * F32(LN2 / SHARPNESS)
        col = i * TILE + lax.broadcasted_iota(jnp.int32, soft.shape, 1)
        soft = jnp.where((col >= 0) & (col < total_rows), soft, 0.0)
        parts = []
        for _ in range(3):
            parts.append(soft.astype(BF16))
            soft = soft - parts[-1].astype(F32)
        parts = jnp.concatenate(parts, axis=0)
        row = i * TILE + lax.broadcasted_iota(jnp.int32, (TILE, LANES), 0)
        n = 2 * videos
        for r in range(rounds):
            first, count = lanes_ref[r : r + 1, :], lanes_ref[rounds + r : rounds + r + 1, :]
            member = jnp.where((row >= first) & (row < first + count), F32(1), F32(0))
            got = dot(parts, member.astype(BF16), ((1,), (0,)))
            out_ref[:, r * LANES : (r + 1) * LANES] += got[:n] + got[n : 2 * n] + got[2 * n :]

    def tile(i, carry):
        w = weights(i)
        collect(i - 1)
        for j, first in enumerate(jobs):
            after = (jobs[j + 1], w) if j + 1 < len(jobs) else (jobs[0], weights(i + 1))
            products(bufs[(j + 1) % 2], *after)
            for v in range(per):
                for col in range(0, TILE, LANES):
                    peak, total = unit(bufs[j % 2], v, col)
                    at = first + v
                    soft_ref[0, at : at + 1, col : col + LANES] = peak
                    soft_ref[1, at : at + 1, col : col + LANES] = total
        return carry

    products(bufs[0], jobs[0], weights(0))
    tiles = (total_rows + TILE - 1) // TILE
    lax.fori_loop(0, tiles, tile, 0)
    collect(tiles - 1)
    for r in range(rounds):
        count = jnp.maximum(lanes_ref[rounds + r : rounds + r + 1, :], 1).astype(F32)
        mean = out_ref[:, r * LANES : (r + 1) * LANES] / count
        near_ref[:, r * LANES : (r + 1) * LANES] = mean[:videos]
        far_ref[:, r * LANES : (r + 1) * LANES] = mean[videos:]


def pair_scores(slots, caps, meta, query, banks):
    line, rounds, rows, width = query.shape
    videos, half = banks[0].shape[:2]
    n_rows = -(-(rounds * line * rows) // TILE) * TILE + TILE + slots
    vmem = pl.BlockSpec(memory_space=pltpu.VMEM)
    anywhere = pl.BlockSpec(memory_space=pl.ANY)
    return pl.pallas_call(
        lambda *refs: score_kernel(slots, caps, *refs),
        in_specs=[pl.BlockSpec(memory_space=pltpu.SMEM), vmem] + [anywhere] * 5,
        out_specs=[vmem] * 2,
        out_shape=[jax.ShapeDtypeStruct((videos, rounds * LANES), F32)] * 2,
        scratch_shapes=[
            pltpu.VMEM(query.shape, query.dtype),
            pltpu.VMEM((2 * videos, 2 * half, width), banks[0].dtype),
            pltpu.VMEM((2 * videos, rounds * LANES), F32),
            pltpu.VMEM((n_rows, width), F32),
            pltpu.VMEM((2, 2 * videos, TILE), F32),
            pltpu.VMEM((2 * videos // JOBS * 2 * half, TILE), F32),
            pltpu.VMEM((2 * videos // JOBS * 2 * half, TILE), F32),
            pltpu.SemaphoreType.DMA((5,)),
        ],
        compiler_params=pltpu.CompilerParams(vmem_limit_bytes=VMEM_BYTES),
        name="soft_scores",
    )(meta, meta, query, *banks)


def prepare_kernel(tok_axis, block_ref, counts_ref, out_ref, piece_ref, count_ref, in_sems, out_sems):
    n, rows = block_ref.shape[0], block_ref.shape[2]
    tok = lax.axis_index(tok_axis)
    lengths = pltpu.make_async_copy(counts_ref, count_ref, in_sems.at[n])
    lengths.start()
    moves = []
    for k in range(n):
        moves.append(
            pltpu.make_async_copy(block_ref.at[k, tok], piece_ref.at[k, pl.ds(0, rows)], in_sems.at[k])
        )
        moves[-1].start()
    lengths.wait()
    counts = jnp.broadcast_to(count_ref[...], (COUNT_ROWS, LANES)).astype(F32).astype(BF16)
    for k in range(n):
        piece_ref[k, rows:, :] = counts
    for k in range(n):
        moves[k].wait()
        moves[k] = pltpu.make_async_copy(piece_ref.at[k], out_ref.at[k], out_sems.at[k])
        moves[k].start()
    for move in moves:
        move.wait()


def pick_kernel(caps, quarters, vid_axis, tok_axis, order_ref, shares_ref, wanted_ref, meta_ref):
    rounds = order_ref.shape[0]
    rows = shares_ref.shape[1] - COUNT_ROWS
    quarter = lax.axis_index(vid_axis) % PAIR * (quarters // PAIR) + lax.axis_index(tok_axis)
    lane = lax.broadcasted_iota(jnp.int32, (1, LANES), 1)
    mine = lane // caps % quarters == quarter
    before = lax.broadcasted_iota(jnp.int32, (LANES, LANES), 0) < lax.broadcasted_iota(
        jnp.int32, (LANES, LANES), 1
    )
    before = jnp.where(before, F32(1), F32(0)).astype(BF16)
    total = jnp.zeros((1, 1), F32)
    meta_ref[...] = jnp.zeros_like(meta_ref)
    for r in range(rounds):
        owner = order_ref[r]
        wanted_ref[r * rows : (r + 1) * rows, :] = shares_ref[owner, :rows, :]
        counts = jnp.where(mine, shares_ref[owner, rows:, :].astype(F32), 0.0)
        starts = dot(counts.astype(BF16), before, ((1,), (0,)))[:1] + total
        counts = counts[:1]
        total = total + jnp.sum(counts, axis=1, keepdims=True)
        meta_ref[r : r + 1, :] = starts.astype(jnp.int32)
        meta_ref[rounds + r : rounds + r + 1, :] = counts.astype(jnp.int32)
    tail = jnp.where(lane == 0, total.astype(jnp.int32), jnp.where(lane == 1, quarter, 0))
    meta_ref[2 * rounds : 2 * rounds + 1, :] = tail


def per_device(captions, caption_lengths, video_bank, owner_order):
    n_vid, n_tok = lax.axis_size("vid"), lax.axis_size("tok")
    capb, slots, width = captions.shape[1:]
    rounds = owner_order.shape[0]
    line = n_vid // PAIR
    caps = capb // (n_vid * n_tok)
    rows = caps * slots
    swap_tok = [(0, 1), (1, 0)]
    swap_pair = [(i, i ^ 1) for i in range(n_vid)]
    swap_both = [
        (i * n_tok + t, (i ^ 1) * n_tok + (t ^ 1)) for i in range(n_vid) for t in range(n_tok)
    ]
    vmem = pl.BlockSpec(memory_space=pltpu.VMEM)
    small = pltpu.CompilerParams(vmem_limit_bytes=VMEM_BYTES)

    tok_bank = lax.ppermute(video_bank, "tok", swap_tok)
    pair_bank = lax.ppermute(video_bank, "vid", swap_pair)
    both_bank = lax.ppermute(tok_bank, "vid", swap_pair)

    pieces = pl.pallas_call(
        lambda *refs: prepare_kernel("tok", *refs),
        in_specs=[pl.BlockSpec(memory_space=pltpu.HBM)] * 2,
        out_specs=pl.BlockSpec(memory_space=pltpu.HBM),
        out_shape=jax.ShapeDtypeStruct((n_vid, rows + COUNT_ROWS, width), captions.dtype),
        scratch_shapes=[
            pltpu.VMEM((n_vid, rows + COUNT_ROWS, width), captions.dtype),
            pltpu.VMEM(caption_lengths.shape, caption_lengths.dtype),
            pltpu.SemaphoreType.DMA((n_vid + 1,)),
            pltpu.SemaphoreType.DMA((n_vid,)),
        ],
        name="prepare",
    )(captions.reshape(n_vid, n_tok, rows, width), caption_lengths)
    shares = lax.all_to_all(pieces, "vid", 0, 0, tiled=True)
    wanted, meta = pl.pallas_call(
        lambda *refs: pick_kernel(caps, PAIR * n_tok, "vid", "tok", *refs),
        in_specs=[pl.BlockSpec(memory_space=pltpu.SMEM), vmem],
        out_specs=[vmem] * 2,
        out_shape=[
            jax.ShapeDtypeStruct((rounds * rows, width), captions.dtype),
            jax.ShapeDtypeStruct((-(-(2 * rounds + 1) // 8) * 8, LANES), jnp.int32),
        ],
        compiler_params=small,
        name="pick",
    )(owner_order, shares)
    lines = [[k * PAIR + s for k in range(line)] for s in range(PAIR)]
    query = lax.all_gather(wanted, "vid", axis=0, axis_index_groups=lines)
    query = query.reshape(line, rounds, rows, width)

    near, far = pair_scores(slots, caps, meta, query, (video_bank, tok_bank, pair_bank, both_bank))
    near = near + lax.ppermute(near, "tok", swap_tok)
    return near + lax.ppermute(far, "vid", swap_pair) + lax.ppermute(far, ("vid", "tok"), swap_both)


def solution(mesh):
    return jax.shard_map(
        per_device,
        mesh=mesh,
        in_specs=(
            P(("groups", "vid"), None, None, None),
            P(("groups", "vid"), None),
            P(("groups", "vid"), "tok", None),
            P("groups"),
        ),
        out_specs=P(("groups", "vid"), None),
        check_vma=False,
    )
```

```python
import jax
import jax.numpy as jnp
from jax import lax
from jax.experimental import pallas as pl
from jax.experimental.pallas import tpu as pltpu
from jax.sharding import PartitionSpec as P

SHARPNESS = 5.0
LOG2E = 1.4426950408889634
LN2 = 0.6931471805599453
COUNT_ROWS = 8
PAIR = 2
STEPS = 4
TILE = 256
LANES = 128
JOBS = 2
VMEM_BYTES = 24 << 20
F32 = jnp.float32
BF16 = jnp.bfloat16


def dot(a, b, dims):
    return lax.dot_general(a, b, (dims, ((), ())), preferred_element_type=F32)


def score_kernel(slots, caps, meta_ref, lanes_ref, q_ref, bank_ref, *refs):
    past, refs = refs[:-7], refs[-7:]
    near_ref, far_ref, out_ref, rows_ref, soft_ref, a_ref, b_ref = refs
    blocks, rounds = q_ref.shape[:2]
    videos, tokens = bank_ref.shape[0] // 2, bank_ref.shape[1]
    total_rows, first_cap, stride = (meta_ref[2 * rounds, k] for k in range(3))

    def pack(i, carry):
        r, g = i // blocks, i % blocks
        piece = q_ref[g, r].astype(F32)
        for c in range(caps):
            start = meta_ref[r, first_cap + g * stride + c]
            rows_ref[pl.ds(start, slots), :] = piece[c * slots : (c + 1) * slots]
        return carry

    lax.fori_loop(0, rounds * blocks, pack, 0)
    out_ref[...] = jnp.zeros_like(out_ref)
    scale = F32(SHARPNESS * LOG2E)
    per = 2 * videos // JOBS
    jobs = [k * per for k in range(JOBS)]
    bufs = (a_ref, b_ref)

    def products(dst, first, w):
        bank = bank_ref[first : first + per].reshape(per * tokens, bank_ref.shape[2])
        dst[...] = dot(jnp.concatenate([bank, bank], axis=1), w, ((1,), (1,)))

    def unit(src, v, col):
        x = src[v * tokens : (v + 1) * tokens, col : col + LANES].reshape(tokens // 8, 8, LANES)
        top = jnp.max(x, axis=0)
        total = jnp.sum(jnp.exp2(x - top[None]), axis=0)
        peak = jnp.max(top, axis=0, keepdims=True)
        return peak, jnp.sum(total * jnp.exp2(top - peak), axis=0, keepdims=True)

    def weights(i):
        q = rows_ref[pl.ds(pl.multiple_of(i * TILE, TILE), TILE), :] * scale
        high = q.astype(BF16)
        return jnp.concatenate([high, (q - high.astype(F32)).astype(BF16)], axis=1)

    def collect(i):
        soft = (soft_ref[0] + jnp.log2(soft_ref[1])) * F32(LN2 / SHARPNESS)
        col = i * TILE + lax.broadcasted_iota(jnp.int32, soft.shape, 1)
        soft = jnp.where((col >= 0) & (col < total_rows), soft, 0.0)
        parts = []
        for _ in range(3):
            parts.append(soft.astype(BF16))
            soft = soft - parts[-1].astype(F32)
        parts = jnp.concatenate(parts, axis=0)
        row = i * TILE + lax.broadcasted_iota(jnp.int32, (TILE, LANES), 0)
        n = 2 * videos
        for r in range(rounds):
            first, count = lanes_ref[r : r + 1, :], lanes_ref[rounds + r : rounds + r + 1, :]
            member = jnp.where((row >= first) & (row < first + count), F32(1), F32(0))
            got = dot(parts, member.astype(BF16), ((1,), (0,)))
            out_ref[:, r * LANES : (r + 1) * LANES] += got[:n] + got[n : 2 * n] + got[2 * n :]

    def tile(i, carry):
        w = weights(i)
        collect(i - 1)
        for j, first in enumerate(jobs):
            after = (jobs[j + 1], w) if j + 1 < len(jobs) else (jobs[0], weights(i + 1))
            products(bufs[(j + 1) % 2], *after)
            for v in range(per):
                for col in range(0, TILE, LANES):
                    peak, total = unit(bufs[j % 2], v, col)
                    at = first + v
                    soft_ref[0, at : at + 1, col : col + LANES] = peak
                    soft_ref[1, at : at + 1, col : col + LANES] = total
        return carry

    products(bufs[0], jobs[0], weights(0))
    tiles = (total_rows + TILE - 1) // TILE
    lax.fori_loop(0, tiles, tile, 0)
    collect(tiles - 1)
    for r in range(rounds):
        count = jnp.maximum(lanes_ref[rounds + r : rounds + r + 1, :], 1).astype(F32)
        mean = out_ref[:, r * LANES : (r + 1) * LANES] / count
        for k, ref in enumerate((near_ref, far_ref)):
            part = mean[k * videos : (k + 1) * videos]
            if past:
                part = part + past[k][:, r * LANES : (r + 1) * LANES]
            ref[:, r * LANES : (r + 1) * LANES] = part


def share_scores(slots, caps, meta, query, bank, *past):
    blocks, rounds, rows, width = query.shape
    videos, tokens = bank.shape[0] // 2, bank.shape[1]
    n_rows = -(-(rounds * blocks * rows) // TILE) * TILE + TILE + slots
    vmem = pl.BlockSpec(memory_space=pltpu.VMEM)
    work = 2 * videos * tokens * rounds * blocks * rows
    return pl.pallas_call(
        lambda *refs: score_kernel(slots, caps, *refs),
        in_specs=[pl.BlockSpec(memory_space=pltpu.SMEM)] + [vmem] * (3 + len(past)),
        out_specs=[vmem] * 2,
        out_shape=[jax.ShapeDtypeStruct((videos, rounds * LANES), F32)] * 2,
        scratch_shapes=[
            pltpu.VMEM((2 * videos, rounds * LANES), F32),
            pltpu.VMEM((n_rows, width), F32),
            pltpu.VMEM((2, 2 * videos, TILE), F32),
            pltpu.VMEM((2 * videos // JOBS * tokens, TILE), F32),
            pltpu.VMEM((2 * videos // JOBS * tokens, TILE), F32),
        ],
        compiler_params=pltpu.CompilerParams(vmem_limit_bytes=VMEM_BYTES),
        cost_estimate=pl.CostEstimate(
            flops=4 * work * width, transcendentals=work, bytes_accessed=bank.size * 2
        ),
        name="soft_scores",
    )(meta, meta, query, bank, *past)


def merge_kernel(own_ref, tok_ref, pair_ref, both_ref, _, out_ref, sems):
    videos, half = own_ref.shape[:2]
    moves = []
    for k, src in enumerate((own_ref, tok_ref, pair_ref, both_ref)):
        dst = out_ref.at[pl.ds(k // 2 * videos, videos), pl.ds(k % 2 * half, half), :]
        moves.append(pltpu.make_async_copy(src, dst, sems.at[k]))
        moves[-1].start()
    for move in moves:
        move.wait()


def prepare_kernel(tok_axis, block_ref, counts_ref, out_ref, piece_ref, count_ref, in_sems, out_sems):
    n, rows = block_ref.shape[0], block_ref.shape[2]
    tok = lax.axis_index(tok_axis)
    lengths = pltpu.make_async_copy(counts_ref, count_ref, in_sems.at[n])
    lengths.start()
    moves = []
    for k in range(n):
        moves.append(
            pltpu.make_async_copy(block_ref.at[k, tok], piece_ref.at[k, pl.ds(0, rows)], in_sems.at[k])
        )
        moves[-1].start()
    lengths.wait()
    counts = jnp.broadcast_to(count_ref[...], (COUNT_ROWS, LANES)).astype(F32).astype(BF16)
    for k in range(n):
        piece_ref[k, rows:, :] = counts
    for k in range(n):
        moves[k].wait()
        moves[k] = pltpu.make_async_copy(piece_ref.at[k], out_ref.at[k], out_sems.at[k])
        moves[k].start()
    for move in moves:
        move.wait()


def pick_kernel(caps, quarters, inner, vid_axis, tok_axis, order_ref, shares_ref, wanted_ref, *metas):
    rounds = order_ref.shape[0]
    rows = shares_ref.shape[1] - COUNT_ROWS
    vid = lax.axis_index(vid_axis)
    quarter = vid % PAIR * (quarters // PAIR) + lax.axis_index(tok_axis)
    place = vid // PAIR % inner
    lane = lax.broadcasted_iota(jnp.int32, (1, LANES), 1)
    before = lax.broadcasted_iota(jnp.int32, (LANES, LANES), 0) < lax.broadcasted_iota(
        jnp.int32, (LANES, LANES), 1
    )
    before = jnp.where(before, F32(1), F32(0)).astype(BF16)
    counts = []
    for r in range(rounds):
        owner = order_ref[r]
        wanted_ref[r * rows : (r + 1) * rows, :] = shares_ref[owner, :rows, :]
        counts.append(shares_ref[owner, rows:, :].astype(F32))
    for k, meta_ref in enumerate(metas):
        block = (place ^ k) * quarters + quarter
        mine = lane // caps % (inner * quarters) == block
        kept = [jnp.where(mine, count, 0.0) for count in counts]
        starts = dot(jnp.concatenate(kept, axis=0).astype(BF16), before, ((1,), (0,)))
        total = jnp.zeros((1, 1), F32)
        meta_ref[...] = jnp.zeros_like(meta_ref)
        for r in range(rounds):
            begin = starts[r * COUNT_ROWS : r * COUNT_ROWS + 1] + total
            total = total + jnp.sum(kept[r][:1], axis=1, keepdims=True)
            meta_ref[r : r + 1, :] = begin.astype(jnp.int32)
            meta_ref[rounds + r : rounds + r + 1, :] = kept[r][:1].astype(jnp.int32)
        tail = jnp.where(lane == 1, block * caps, jnp.where(lane == 2, inner * quarters * caps, 0))
        tail = jnp.where(lane == 0, total.astype(jnp.int32), tail)
        meta_ref[2 * rounds : 2 * rounds + 1, :] = tail


def per_device(captions, caption_lengths, video_bank, owner_order):
    n_vid, n_tok = lax.axis_size("vid"), lax.axis_size("tok")
    capb, slots, width = captions.shape[1:]
    rounds = owner_order.shape[0]
    videos, half = video_bank.shape[:2]
    line = n_vid // PAIR
    caps = capb // (n_vid * n_tok)
    rows = caps * slots
    swap_tok = [(0, 1), (1, 0)]
    swap_pair = [(i, i ^ 1) for i in range(n_vid)]
    swap_both = [
        (i * n_tok + t, (i ^ 1) * n_tok + (t ^ 1)) for i in range(n_vid) for t in range(n_tok)
    ]
    vmem = pl.BlockSpec(memory_space=pltpu.VMEM)
    small = pltpu.CompilerParams(vmem_limit_bytes=VMEM_BYTES)

    tok_bank = lax.ppermute(video_bank, "tok", swap_tok)
    pair_bank = lax.ppermute(video_bank, "vid", swap_pair)
    both_bank = lax.ppermute(tok_bank, "vid", swap_pair)

    pieces = pl.pallas_call(
        lambda *refs: prepare_kernel("tok", *refs),
        in_specs=[pl.BlockSpec(memory_space=pltpu.HBM)] * 2,
        out_specs=pl.BlockSpec(memory_space=pltpu.HBM),
        out_shape=jax.ShapeDtypeStruct((n_vid, rows + COUNT_ROWS, width), captions.dtype),
        scratch_shapes=[
            pltpu.VMEM((n_vid, rows + COUNT_ROWS, width), captions.dtype),
            pltpu.VMEM(caption_lengths.shape, caption_lengths.dtype),
            pltpu.SemaphoreType.DMA((n_vid + 1,)),
            pltpu.SemaphoreType.DMA((n_vid,)),
        ],
        name="prepare",
    )(captions.reshape(n_vid, n_tok, rows, width), caption_lengths)
    shares = lax.all_to_all(pieces, "vid", 0, 0, tiled=True)
    inner = min(STEPS, line)
    wanted, *metas = pl.pallas_call(
        lambda *refs: pick_kernel(caps, PAIR * n_tok, inner, "vid", "tok", *refs),
        in_specs=[pl.BlockSpec(memory_space=pltpu.SMEM), vmem],
        out_specs=[vmem] * (1 + inner),
        out_shape=[jax.ShapeDtypeStruct((rounds * rows, width), captions.dtype)]
        + [jax.ShapeDtypeStruct((-(-(2 * rounds + 1) // 8) * 8, LANES), jnp.int32)] * inner,
        compiler_params=small,
        name="pick",
    )(owner_order, shares)
    blocks = line // inner
    if blocks > 1:
        groups = [
            [(b * inner + m) * PAIR + s for b in range(blocks)] for m in range(inner) for s in range(PAIR)
        ]
        wanted = lax.all_gather(wanted, "vid", axis=0, axis_index_groups=groups)
    wanted = wanted.reshape(blocks, rounds, rows, width)
    arrived = [wanted]
    for k in range(1, inner):
        steps = [(i, i ^ (k * PAIR)) for i in range(n_vid)]
        arrived.append(lax.ppermute(wanted, "vid", steps))

    bank = pl.pallas_call(
        merge_kernel,
        in_specs=[pl.BlockSpec(memory_space=pl.ANY)] * 5,
        out_specs=vmem,
        out_shape=jax.ShapeDtypeStruct((2 * videos, 2 * half, width), video_bank.dtype),
        scratch_shapes=[pltpu.SemaphoreType.DMA((4,))],
        compiler_params=small,
        name="merge",
    )(video_bank, tok_bank, pair_bank, both_bank, metas[0])
    scores = ()
    for meta, query in zip(metas, arrived):
        scores = share_scores(slots, caps, meta, query, bank, *scores)
    near, far = scores
    near = near + lax.ppermute(near, "tok", swap_tok)
    return near + lax.ppermute(far, "vid", swap_pair) + lax.ppermute(far, ("vid", "tok"), swap_both)


def solution(mesh):
    return jax.shard_map(
        per_device,
        mesh=mesh,
        in_specs=(
            P(("groups", "vid"), None, None, None),
            P(("groups", "vid"), None),
            P(("groups", "vid"), "tok", None),
            P("groups"),
        ),
        out_specs=P(("groups", "vid"), None),
        check_vma=False,
    )
```

```python
import functools

import jax
import jax.numpy as jnp
from jax import lax
from jax.experimental import pallas as pl
from jax.experimental.pallas import tpu as pltpu
from jax.sharding import PartitionSpec as P


SHARPNESS = 5.0
LOG2E = 1.4426950408889634
LN2 = 0.6931471805599453
COUNT_ROWS = 8
PAIR = 2
STEPS = 4
TILE = 256
LANES = 128
FIRST_JOB = 2
LEAST = 2.0**-90
MOST = 2.0**120
VMEM_BYTES = 24 << 20
F32 = jnp.float32
BF16 = jnp.bfloat16


def dot(a, b, dims):
    return lax.dot_general(a, b, (dims, ((), ())), preferred_element_type=F32)


def thirds(x):
    parts = []
    for _ in range(3):
        parts.append(x.astype(BF16))
        x = x - parts[-1].astype(F32)
    return parts


def score_kernel(slots, caps, share, last, meta_ref, lanes_ref, q_ref, bank_ref, *refs):
    past, refs = (refs[:1], refs[1:]) if share else ((), refs)
    outs, refs = refs[: 1 + last], refs[1 + last :]
    out_ref, (rows_ref, soft_ref, bad_ref, a_ref, b_ref) = refs[0] if last else outs[0], refs[last:]
    blocks, rounds = q_ref.shape[:2]
    videos, tokens = bank_ref.shape[0] // 2, bank_ref.shape[1]
    total_rows = meta_ref[3, share]

    def pack(i, carry):
        r, g = i // blocks, i % blocks
        piece = q_ref[g, r].astype(F32)
        for c in range(caps):
            start = meta_ref[0, (share * rounds * blocks + i) * caps + c]
            rows_ref[pl.ds(start, slots), :] = piece[c * slots : (c + 1) * slots]
        return carry

    lax.fori_loop(0, rounds * blocks, pack, 0)
    lane = lax.broadcasted_iota(jnp.int32, (1, LANES), 1)
    here = lane // (rounds * blocks * caps) == share
    first = lanes_ref[0:1, :]
    end = jnp.where(here, first + lanes_ref[1:2, :], 0)
    scale = F32(SHARPNESS * LOG2E)
    jobs = [(0, FIRST_JOB), (FIRST_JOB, 2 * videos - FIRST_JOB)]
    bufs = (a_ref, b_ref)

    def products(dst, job, w):
        first, size = job
        bank = bank_ref[first : first + size].reshape(size * tokens, bank_ref.shape[2])
        dst[...] = dot(jnp.concatenate([bank, bank], axis=1), w, ((1,), (1,)))

    def unit(src, v, col, shifted):
        x = src[v * tokens : (v + 1) * tokens, col : col + LANES].reshape(tokens // 8, 8, LANES)
        if not shifted:
            return None, jnp.sum(jnp.sum(jnp.exp2(x), axis=0), axis=0, keepdims=True)
        top = jnp.max(x, axis=0)
        total = jnp.sum(jnp.exp2(x - top[None]), axis=0)
        peak = jnp.max(top, axis=0, keepdims=True)
        return peak, jnp.sum(total * jnp.exp2(top - peak), axis=0, keepdims=True)

    def weights(i):
        q = rows_ref[pl.ds(pl.multiple_of(i * TILE, TILE), TILE), :] * scale
        high = q.astype(BF16)
        return jnp.concatenate([high, (q - high.astype(F32)).astype(BF16)], axis=1)

    def collect(i, shifted):
        sums = soft_ref[1]
        soft = jnp.log2(sums)
        if shifted:
            soft = soft + soft_ref[0]
        col = i * TILE + lax.broadcasted_iota(jnp.int32, soft.shape, 1)
        valid = (col >= 0) & (col < total_rows)
        if not shifted:
            fine = (sums > LEAST) & (sums < MOST)
            bad_ref[...] = jnp.where(valid & ~fine, 1.0, bad_ref[...])
        soft = jnp.where(valid, soft * F32(LN2 / SHARPNESS), 0.0)
        parts = jnp.concatenate(thirds(soft), axis=0)
        row = i * TILE + lax.broadcasted_iota(jnp.int32, (TILE, LANES), 0)
        n = 2 * videos
        member = jnp.where((row >= first) & (row < end), F32(1), F32(0))
        got = dot(parts, member.astype(BF16), ((1,), (0,)))
        out_ref[...] += got[:n] + got[n : 2 * n] + got[2 * n :]

    def tile(shifted, i, carry):
        w = weights(i)
        collect(i - 1, shifted)
        for j, (base, size) in enumerate(jobs):
            after = (jobs[j + 1], w) if j + 1 < len(jobs) else (jobs[0], weights(i + 1))
            products(bufs[(j + 1) % 2], *after)
            for v in range(size):
                for col in range(0, TILE, LANES):
                    peak, total = unit(bufs[j % 2], v, col, shifted)
                    at = base + v
                    if shifted:
                        soft_ref[0, at : at + 1, col : col + LANES] = peak
                    soft_ref[1, at : at + 1, col : col + LANES] = total
        return carry

    tiles = (total_rows + TILE - 1) // TILE

    def run(shifted):
        out_ref[...] = past[0][...] if past else jnp.zeros_like(out_ref)
        products(bufs[0], jobs[0], weights(0))
        lax.fori_loop(0, tiles, functools.partial(tile, shifted), 0)
        collect(tiles - 1, shifted)

    bad_ref[...] = jnp.zeros_like(bad_ref)
    run(False)

    @pl.when(jnp.max(bad_ref[...]) > 0)
    def _():
        run(True)

    if last:
        mean = out_ref[...] / jnp.maximum(lanes_ref[1:2, :], 1).astype(F32)
        column = lax.broadcasted_iota(jnp.int32, (rounds * LANES, LANES), 0)
        spread = jnp.where(column == lanes_ref[2:3, :], F32(1), F32(0)).astype(BF16)
        n = 2 * videos
        got = dot(jnp.concatenate(thirds(mean), axis=0), spread, ((1,), (1,)))
        got = got[:n] + got[n : 2 * n] + got[2 * n :]
        outs[0][...] = got[:videos]
        outs[1][...] = got[videos:]


def share_scores(slots, caps, share, last, meta, query, bank, *past):
    blocks, rounds, rows, width = query.shape
    videos, tokens = bank.shape[0] // 2, bank.shape[1]
    n_rows = -(-(rounds * blocks * rows) // TILE) * TILE + TILE + slots
    vmem = pl.BlockSpec(memory_space=pltpu.VMEM)
    work = 2 * videos * tokens * rounds * blocks * rows
    total = (2 * videos, LANES)
    outs = [(videos, rounds * LANES)] * 2 if last else [total]
    return pl.pallas_call(
        lambda *refs: score_kernel(slots, caps, share, last, *refs),
        in_specs=[pl.BlockSpec(memory_space=pltpu.SMEM)] + [vmem] * (3 + len(past)),
        out_specs=[vmem] * len(outs),
        out_shape=[jax.ShapeDtypeStruct(shape, F32) for shape in outs],
        scratch_shapes=[pltpu.VMEM(total, F32)] * last
        + [
            pltpu.VMEM((n_rows, width), F32),
            pltpu.VMEM((2, 2 * videos, TILE), F32),
            pltpu.VMEM((2 * videos, TILE), F32),
            pltpu.VMEM((FIRST_JOB * tokens, TILE), F32),
            pltpu.VMEM(((2 * videos - FIRST_JOB) * tokens, TILE), F32),
        ],
        compiler_params=pltpu.CompilerParams(vmem_limit_bytes=VMEM_BYTES),
        cost_estimate=pl.CostEstimate(
            flops=4 * work * width, transcendentals=work, bytes_accessed=bank.size * 2
        ),
        name="soft_scores",
    )(meta, meta, query, bank, *past)


def merge_kernel(caps, blocks, inner, quarters, vid_axis, tok_axis, order_ref, own_ref, tok_ref,
                 pair_ref, both_ref, counts_ref, bank_ref, meta_ref, sems):
    videos, half = own_ref.shape[:2]
    rounds = order_ref.shape[0]
    moves = []
    for k, src in enumerate((own_ref, tok_ref, pair_ref, both_ref)):
        dst = bank_ref.at[pl.ds(k // 2 * videos, videos), pl.ds(k % 2 * half, half), :]
        moves.append(pltpu.make_async_copy(src, dst, sems.at[k]))
        moves[-1].start()
    vid = lax.axis_index(vid_axis)
    quarter = vid % PAIR * (quarters // PAIR) + lax.axis_index(tok_axis)
    place = vid // PAIR % inner
    per = rounds * blocks * caps

    def where(lane):
        share, rest = lane // per, lane % per
        block = rest // caps % blocks * inner + (share ^ place)
        return share, rest // (blocks * caps), (block * quarters + quarter) * caps + lane % caps

    down = lax.broadcasted_iota(jnp.int32, (LANES, LANES), 0)
    across = lax.broadcasted_iota(jnp.int32, (LANES, LANES), 1)
    share, turn, cap = where(lax.broadcasted_iota(jnp.int32, (1, LANES), 1))
    used = share < inner
    counts = jnp.zeros((COUNT_ROWS, LANES), F32)
    for r in range(rounds):
        pick = jnp.where((down == cap) & (turn == r) & used, F32(1), F32(0)).astype(BF16)
        counts = counts + dot(counts_ref[r], pick, ((1,), (0,)))
    before = jnp.where((down < across) & (down // per == share), F32(1), F32(0)).astype(BF16)
    within = jnp.where(down // per == across, F32(1), F32(0)).astype(BF16)
    starts = dot(counts.astype(BF16), before, ((1,), (0,)))
    totals = dot(counts.astype(BF16), within, ((1,), (0,)))
    meta_ref[...] = jnp.zeros_like(meta_ref)
    meta_ref[0:1, :] = starts[:1].astype(jnp.int32)
    meta_ref[1:2, :] = counts[:1].astype(jnp.int32)
    meta_ref[2:3, :] = jnp.where(used, turn * LANES + cap, -1)
    meta_ref[3:4, :] = totals[:1].astype(jnp.int32)
    for move in moves:
        move.wait()


def prepare_kernel(tok_axis, block_ref, counts_ref, out_ref, piece_ref, count_ref, in_sems, out_sems):
    n, rows = block_ref.shape[0], block_ref.shape[2]
    tok = lax.axis_index(tok_axis)
    lengths = pltpu.make_async_copy(counts_ref, count_ref, in_sems.at[n])
    lengths.start()
    moves = []
    for k in range(n):
        moves.append(
            pltpu.make_async_copy(block_ref.at[k, tok], piece_ref.at[k, pl.ds(0, rows)], in_sems.at[k])
        )
        moves[-1].start()
    lengths.wait()
    counts = jnp.broadcast_to(count_ref[...], (COUNT_ROWS, LANES)).astype(F32).astype(BF16)
    for k in range(n):
        piece_ref[k, rows:, :] = counts
    for k in range(n):
        moves[k].wait()
        moves[k] = pltpu.make_async_copy(piece_ref.at[k], out_ref.at[k], out_sems.at[k])
        moves[k].start()
    for move in moves:
        move.wait()


def pick_kernel(order_ref, shares_ref, wanted_ref, counts_ref):
    rows = shares_ref.shape[1] - COUNT_ROWS
    for r in range(order_ref.shape[0]):
        owner = order_ref[r]
        wanted_ref[r * rows : (r + 1) * rows, :] = shares_ref[owner, :rows, :]
        counts_ref[r] = shares_ref[owner, rows:, :]


def per_device(captions, caption_lengths, video_bank, owner_order):
    n_vid, n_tok = lax.axis_size("vid"), lax.axis_size("tok")
    capb, slots, width = captions.shape[1:]
    rounds = owner_order.shape[0]
    videos, half = video_bank.shape[:2]
    line = n_vid // PAIR
    caps = capb // (n_vid * n_tok)
    rows = caps * slots
    swap_tok = [(0, 1), (1, 0)]
    swap_pair = [(i, i ^ 1) for i in range(n_vid)]
    swap_both = [
        (i * n_tok + t, (i ^ 1) * n_tok + (t ^ 1)) for i in range(n_vid) for t in range(n_tok)
    ]
    vmem = pl.BlockSpec(memory_space=pltpu.VMEM)
    small = pltpu.CompilerParams(vmem_limit_bytes=VMEM_BYTES)

    tok_bank = lax.ppermute(video_bank, "tok", swap_tok)
    pair_bank = lax.ppermute(video_bank, "vid", swap_pair)

    pieces = pl.pallas_call(
        lambda *refs: prepare_kernel("tok", *refs),
        in_specs=[pl.BlockSpec(memory_space=pltpu.HBM)] * 2,
        out_specs=pl.BlockSpec(memory_space=pltpu.HBM),
        out_shape=jax.ShapeDtypeStruct((n_vid, rows + COUNT_ROWS, width), captions.dtype),
        scratch_shapes=[
            pltpu.VMEM((n_vid, rows + COUNT_ROWS, width), captions.dtype),
            pltpu.VMEM(caption_lengths.shape, caption_lengths.dtype),
            pltpu.SemaphoreType.DMA((n_vid + 1,)),
            pltpu.SemaphoreType.DMA((n_vid,)),
        ],
        name="prepare",
    )(captions.reshape(n_vid, n_tok, rows, width), caption_lengths)
    shares = lax.all_to_all(pieces, "vid", 0, 0, tiled=True)
    wanted, counts = pl.pallas_call(
        pick_kernel,
        in_specs=[pl.BlockSpec(memory_space=pltpu.SMEM), vmem],
        out_specs=[vmem] * 2,
        out_shape=[
            jax.ShapeDtypeStruct((rounds * rows, width), captions.dtype),
            jax.ShapeDtypeStruct((rounds, COUNT_ROWS, width), captions.dtype),
        ],
        compiler_params=small,
        name="pick",
    )(owner_order, shares)
    inner = min(STEPS, line)
    blocks = line // inner
    if blocks > 1:
        groups = [
            [(b * inner + m) * PAIR + s for b in range(blocks)] for m in range(inner) for s in range(PAIR)
        ]
        wanted = lax.all_gather(wanted, "vid", axis=0, axis_index_groups=groups)
    wanted = wanted.reshape(blocks, rounds, rows, width)
    arrived = [wanted]
    for k in range(1, inner):
        steps = [(i, i ^ (k * PAIR)) for i in range(n_vid)]
        arrived.append(lax.ppermute(wanted, "vid", steps))

    both_bank = lax.ppermute(pair_bank, "tok", swap_tok)
    bank, meta = pl.pallas_call(
        lambda *refs: merge_kernel(caps, blocks, inner, PAIR * n_tok, "vid", "tok", *refs),
        in_specs=[pl.BlockSpec(memory_space=pltpu.SMEM)]
        + [pl.BlockSpec(memory_space=pl.ANY)] * 4
        + [vmem],
        out_specs=[vmem] * 2,
        out_shape=[
            jax.ShapeDtypeStruct((2 * videos, 2 * half, width), video_bank.dtype),
            jax.ShapeDtypeStruct((8, LANES), jnp.int32),
        ],
        scratch_shapes=[pltpu.SemaphoreType.DMA((4,))],
        compiler_params=small,
        name="merge",
    )(owner_order, video_bank, tok_bank, pair_bank, both_bank, counts)
    total = ()
    for k, query in enumerate(arrived):
        total = share_scores(slots, caps, k, k == inner - 1, meta, query, bank, *total)
    near, far = total
    near = near + lax.ppermute(near, "tok", swap_tok)
    return near + lax.ppermute(far, "vid", swap_pair) + lax.ppermute(far, ("vid", "tok"), swap_both)


def solution(mesh):
    return jax.shard_map(
        per_device,
        mesh=mesh,
        in_specs=(
            P(("groups", "vid"), None, None, None),
            P(("groups", "vid"), None),
            P(("groups", "vid"), "tok", None),
            P("groups"),
        ),
        out_specs=P(("groups", "vid"), None),
        check_vma=False,
    )
```

```python
import functools

import jax
import jax.numpy as jnp
from jax import lax
from jax.experimental import pallas as pl
from jax.experimental.pallas import tpu as pltpu
from jax.sharding import PartitionSpec as P


SHARPNESS = 5.0
LOG2E = 1.4426950408889634
LN2 = 0.6931471805599453
COUNT_ROWS = 8
PAIR = 2
STEPS = 4
TILE = 256
LANES = 128
FIRST_JOB = 2
LEAST = 2.0**-90
MOST = 2.0**120
VMEM_BYTES = 24 << 20
F32 = jnp.float32
BF16 = jnp.bfloat16


def dot(a, b, dims):
    return lax.dot_general(a, b, (dims, ((), ())), preferred_element_type=F32)


def thirds(x):
    parts = []
    for _ in range(3):
        parts.append(x.astype(BF16))
        x = x - parts[-1].astype(F32)
    return parts


def score_kernel(slots, caps, share, last, meta_ref, lanes_ref, q_ref, bank_ref, *refs):
    past, refs = (refs[:1], refs[1:]) if share else ((), refs)
    outs, refs = refs[: 1 + last], refs[1 + last :]
    out_ref, (rows_ref, soft_ref, bad_ref, a_ref, b_ref) = refs[0] if last else outs[0], refs[last:]
    blocks, rounds = q_ref.shape[:2]
    videos, tokens = bank_ref.shape[0] // 2, bank_ref.shape[1]
    total_rows = meta_ref[3, share]

    def pack(i, carry):
        r, g = i // blocks, i % blocks
        piece = q_ref[g, r].astype(F32)
        for c in range(caps):
            start = meta_ref[0, (share * rounds * blocks + i) * caps + c]
            rows_ref[pl.ds(start, slots), :] = piece[c * slots : (c + 1) * slots]
        return carry

    lax.fori_loop(0, rounds * blocks, pack, 0)
    lane = lax.broadcasted_iota(jnp.int32, (1, LANES), 1)
    here = lane // (rounds * blocks * caps) == share
    first = lanes_ref[0:1, :]
    end = jnp.where(here, first + lanes_ref[1:2, :], 0)
    scale = F32(SHARPNESS * LOG2E)
    jobs = [(0, FIRST_JOB), (FIRST_JOB, 2 * videos - FIRST_JOB)]
    bufs = (a_ref, b_ref)

    def products(dst, job, w):
        first, size = job
        bank = bank_ref[first : first + size].reshape(size * tokens, bank_ref.shape[2])
        dst[...] = dot(jnp.concatenate([bank, bank], axis=1), w, ((1,), (1,)))

    def unit(src, v, col, shifted):
        x = src[v * tokens : (v + 1) * tokens, col : col + LANES].reshape(tokens // 8, 8, LANES)
        if not shifted:
            return None, jnp.sum(jnp.sum(jnp.exp2(x), axis=0), axis=0, keepdims=True)
        top = jnp.max(x, axis=0)
        total = jnp.sum(jnp.exp2(x - top[None]), axis=0)
        peak = jnp.max(top, axis=0, keepdims=True)
        return peak, jnp.sum(total * jnp.exp2(top - peak), axis=0, keepdims=True)

    def weights(i):
        q = rows_ref[pl.ds(pl.multiple_of(i * TILE, TILE), TILE), :] * scale
        high = q.astype(BF16)
        return jnp.concatenate([high, (q - high.astype(F32)).astype(BF16)], axis=1)

    def collect(i, shifted):
        sums = soft_ref[1]
        soft = jnp.log2(sums)
        if shifted:
            soft = soft + soft_ref[0]
        col = i * TILE + lax.broadcasted_iota(jnp.int32, soft.shape, 1)
        valid = (col >= 0) & (col < total_rows)
        if not shifted:
            fine = (sums > LEAST) & (sums < MOST)
            bad_ref[...] = jnp.where(valid & ~fine, 1.0, bad_ref[...])
        soft = jnp.where(valid, soft * F32(LN2 / SHARPNESS), 0.0)
        parts = jnp.concatenate(thirds(soft), axis=0)
        row = i * TILE + lax.broadcasted_iota(jnp.int32, (TILE, LANES), 0)
        n = 2 * videos
        member = jnp.where((row >= first) & (row < end), F32(1), F32(0))
        got = dot(parts, member.astype(BF16), ((1,), (0,)))
        out_ref[...] += got[:n] + got[n : 2 * n] + got[2 * n :]

    def tile(shifted, i, carry):
        w = weights(i)
        collect(i - 1, shifted)
        for j, (base, size) in enumerate(jobs):
            after = (jobs[j + 1], w) if j + 1 < len(jobs) else (jobs[0], weights(i + 1))
            products(bufs[(j + 1) % 2], *after)
            for v in range(size):
                for col in range(0, TILE, LANES):
                    peak, total = unit(bufs[j % 2], v, col, shifted)
                    at = base + v
                    if shifted:
                        soft_ref[0, at : at + 1, col : col + LANES] = peak
                    soft_ref[1, at : at + 1, col : col + LANES] = total
        return carry

    tiles = (total_rows + TILE - 1) // TILE

    def run(shifted):
        out_ref[...] = past[0][...] if past else jnp.zeros_like(out_ref)
        products(bufs[0], jobs[0], weights(0))
        lax.fori_loop(0, tiles, functools.partial(tile, shifted), 0)
        collect(tiles - 1, shifted)

    bad_ref[...] = jnp.zeros_like(bad_ref)
    run(False)

    @pl.when(jnp.max(bad_ref[...]) > 0)
    def _():
        run(True)

    if last:
        mean = out_ref[...] / jnp.maximum(lanes_ref[1:2, :], 1).astype(F32)
        column = lax.broadcasted_iota(jnp.int32, (rounds * LANES, LANES), 0)
        spread = jnp.where(column == lanes_ref[2:3, :], F32(1), F32(0)).astype(BF16)
        n = 2 * videos
        got = dot(jnp.concatenate(thirds(mean), axis=0), spread, ((1,), (1,)))
        got = got[:n] + got[n : 2 * n] + got[2 * n :]
        outs[0][...] = got[:videos]
        outs[1][...] = got[videos:]


def share_scores(slots, caps, share, last, meta, query, bank, *past):
    blocks, rounds, rows, width = query.shape
    videos, tokens = bank.shape[0] // 2, bank.shape[1]
    n_rows = -(-(rounds * blocks * rows) // TILE) * TILE + TILE + slots
    vmem = pl.BlockSpec(memory_space=pltpu.VMEM)
    work = 2 * videos * tokens * rounds * blocks * rows
    total = (2 * videos, LANES)
    outs = [(videos, rounds * LANES)] * 2 if last else [total]
    return pl.pallas_call(
        lambda *refs: score_kernel(slots, caps, share, last, *refs),
        in_specs=[pl.BlockSpec(memory_space=pltpu.SMEM)] + [vmem] * (3 + len(past)),
        out_specs=[vmem] * len(outs),
        out_shape=[jax.ShapeDtypeStruct(shape, F32) for shape in outs],
        scratch_shapes=[pltpu.VMEM(total, F32)] * last
        + [
            pltpu.VMEM((n_rows, width), F32),
            pltpu.VMEM((2, 2 * videos, TILE), F32),
            pltpu.VMEM((2 * videos, TILE), F32),
            pltpu.VMEM((FIRST_JOB * tokens, TILE), F32),
            pltpu.VMEM(((2 * videos - FIRST_JOB) * tokens, TILE), F32),
        ],
        compiler_params=pltpu.CompilerParams(vmem_limit_bytes=VMEM_BYTES),
        cost_estimate=pl.CostEstimate(
            flops=4 * work * width, transcendentals=work, bytes_accessed=bank.size * 2
        ),
        name="soft_scores",
    )(meta, meta, query, bank, *past)


def merge_kernel(own_ref, tok_ref, pair_ref, both_ref, bank_ref, sems):
    videos, half = own_ref.shape[:2]
    moves = []
    for k, src in enumerate((own_ref, tok_ref, pair_ref, both_ref)):
        dst = bank_ref.at[pl.ds(k // 2 * videos, videos), pl.ds(k % 2 * half, half), :]
        moves.append(pltpu.make_async_copy(src, dst, sems.at[k]))
        moves[-1].start()
    for move in moves:
        move.wait()


def tables_kernel(caps, blocks, inner, quarters, vid_axis, tok_axis, counts_ref, meta_ref):
    rounds = counts_ref.shape[0]
    vid = lax.axis_index(vid_axis)
    quarter = vid % PAIR * (quarters // PAIR) + lax.axis_index(tok_axis)
    place = vid // PAIR % inner
    per = rounds * blocks * caps

    def where(lane):
        share, rest = lane // per, lane % per
        block = rest // caps % blocks * inner + (share ^ place)
        return share, rest // (blocks * caps), (block * quarters + quarter) * caps + lane % caps

    down = lax.broadcasted_iota(jnp.int32, (LANES, LANES), 0)
    across = lax.broadcasted_iota(jnp.int32, (LANES, LANES), 1)
    share, turn, cap = where(lax.broadcasted_iota(jnp.int32, (1, LANES), 1))
    used = share < inner
    counts = jnp.zeros((COUNT_ROWS, LANES), F32)
    for r in range(rounds):
        pick = jnp.where((down == cap) & (turn == r) & used, F32(1), F32(0)).astype(BF16)
        counts = counts + dot(counts_ref[r], pick, ((1,), (0,)))
    before = jnp.where((down < across) & (down // per == share), F32(1), F32(0)).astype(BF16)
    within = jnp.where(down // per == across, F32(1), F32(0)).astype(BF16)
    starts = dot(counts.astype(BF16), before, ((1,), (0,)))
    totals = dot(counts.astype(BF16), within, ((1,), (0,)))
    meta_ref[...] = jnp.zeros_like(meta_ref)
    meta_ref[0:1, :] = starts[:1].astype(jnp.int32)
    meta_ref[1:2, :] = counts[:1].astype(jnp.int32)
    meta_ref[2:3, :] = jnp.where(used, turn * LANES + cap, -1)
    meta_ref[3:4, :] = totals[:1].astype(jnp.int32)


def prepare_kernel(tok_axis, block_ref, counts_ref, out_ref, piece_ref, count_ref, in_sems, out_sems):
    n, rows = block_ref.shape[0], block_ref.shape[2]
    tok = lax.axis_index(tok_axis)
    lengths = pltpu.make_async_copy(counts_ref, count_ref, in_sems.at[n])
    lengths.start()
    moves = []
    for k in range(n):
        moves.append(
            pltpu.make_async_copy(block_ref.at[k, tok], piece_ref.at[k, pl.ds(0, rows)], in_sems.at[k])
        )
        moves[-1].start()
    lengths.wait()
    counts = jnp.broadcast_to(count_ref[...], (COUNT_ROWS, LANES)).astype(F32).astype(BF16)
    for k in range(n):
        piece_ref[k, rows:, :] = counts
    for k in range(n):
        moves[k].wait()
        moves[k] = pltpu.make_async_copy(piece_ref.at[k], out_ref.at[k], out_sems.at[k])
        moves[k].start()
    for move in moves:
        move.wait()


def pick_kernel(order_ref, shares_ref, wanted_ref, counts_ref):
    rows = shares_ref.shape[1] - COUNT_ROWS
    for r in range(order_ref.shape[0]):
        owner = order_ref[r]
        wanted_ref[r * rows : (r + 1) * rows, :] = shares_ref[owner, :rows, :]
        counts_ref[r] = shares_ref[owner, rows:, :]


def per_device(captions, caption_lengths, video_bank, owner_order):
    n_vid, n_tok = lax.axis_size("vid"), lax.axis_size("tok")
    capb, slots, width = captions.shape[1:]
    rounds = owner_order.shape[0]
    videos, half = video_bank.shape[:2]
    line = n_vid // PAIR
    caps = capb // (n_vid * n_tok)
    rows = caps * slots
    swap_tok = [(0, 1), (1, 0)]
    swap_pair = [(i, i ^ 1) for i in range(n_vid)]
    swap_both = [
        (i * n_tok + t, (i ^ 1) * n_tok + (t ^ 1)) for i in range(n_vid) for t in range(n_tok)
    ]
    vmem = pl.BlockSpec(memory_space=pltpu.VMEM)
    small = pltpu.CompilerParams(vmem_limit_bytes=VMEM_BYTES)

    tok_bank = lax.ppermute(video_bank, "tok", swap_tok)
    pair_bank = lax.ppermute(video_bank, "vid", swap_pair)
    both_bank = lax.ppermute(pair_bank, "tok", swap_tok)

    pieces = pl.pallas_call(
        lambda *refs: prepare_kernel("tok", *refs),
        in_specs=[pl.BlockSpec(memory_space=pltpu.HBM)] * 2,
        out_specs=pl.BlockSpec(memory_space=pltpu.HBM),
        out_shape=jax.ShapeDtypeStruct((n_vid, rows + COUNT_ROWS, width), captions.dtype),
        scratch_shapes=[
            pltpu.VMEM((n_vid, rows + COUNT_ROWS, width), captions.dtype),
            pltpu.VMEM(caption_lengths.shape, caption_lengths.dtype),
            pltpu.SemaphoreType.DMA((n_vid + 1,)),
            pltpu.SemaphoreType.DMA((n_vid,)),
        ],
        name="prepare",
    )(captions.reshape(n_vid, n_tok, rows, width), caption_lengths)
    shares = lax.all_to_all(pieces, "vid", 0, 0, tiled=True)
    bank = pl.pallas_call(
        merge_kernel,
        in_specs=[pl.BlockSpec(memory_space=pl.ANY)] * 4,
        out_specs=vmem,
        out_shape=jax.ShapeDtypeStruct((2 * videos, 2 * half, width), video_bank.dtype),
        scratch_shapes=[pltpu.SemaphoreType.DMA((4,))],
        compiler_params=small,
        name="merge",
    )(video_bank, tok_bank, pair_bank, both_bank)
    wanted, counts = pl.pallas_call(
        pick_kernel,
        in_specs=[pl.BlockSpec(memory_space=pltpu.SMEM), vmem],
        out_specs=[vmem] * 2,
        out_shape=[
            jax.ShapeDtypeStruct((rounds * rows, width), captions.dtype),
            jax.ShapeDtypeStruct((rounds, COUNT_ROWS, width), captions.dtype),
        ],
        compiler_params=small,
        name="pick",
    )(owner_order, shares)
    inner = min(STEPS, line)
    blocks = line // inner
    if blocks > 1:
        groups = [
            [(b * inner + m) * PAIR + s for b in range(blocks)] for m in range(inner) for s in range(PAIR)
        ]
        wanted = lax.all_gather(wanted, "vid", axis=0, axis_index_groups=groups)
    wanted = wanted.reshape(blocks, rounds, rows, width)
    arrived = [wanted]
    for k in range(1, inner):
        steps = [(i, i ^ (k * PAIR)) for i in range(n_vid)]
        arrived.append(lax.ppermute(wanted, "vid", steps))

    meta = pl.pallas_call(
        lambda *refs: tables_kernel(caps, blocks, inner, PAIR * n_tok, "vid", "tok", *refs),
        in_specs=[vmem],
        out_specs=vmem,
        out_shape=jax.ShapeDtypeStruct((8, LANES), jnp.int32),
        compiler_params=small,
        name="tables",
    )(counts)
    total = ()
    for k, query in enumerate(arrived):
        total = share_scores(slots, caps, k, k == inner - 1, meta, query, bank, *total)
    near, far = total
    near = near + lax.ppermute(near, "tok", swap_tok)
    return near + lax.ppermute(far, "vid", swap_pair) + lax.ppermute(far, ("vid", "tok"), swap_both)


def solution(mesh):
    return jax.shard_map(
        per_device,
        mesh=mesh,
        in_specs=(
            P(("groups", "vid"), None, None, None),
            P(("groups", "vid"), None),
            P(("groups", "vid"), "tok", None),
            P("groups"),
        ),
        out_specs=P(("groups", "vid"), None),
        check_vma=False,
    )
```

```python
import functools

import jax
import jax.numpy as jnp
from jax import lax
from jax.experimental import pallas as pl
from jax.experimental.pallas import tpu as pltpu
from jax.sharding import PartitionSpec as P


SHARPNESS = 5.0
LOG2E = 1.4426950408889634
LN2 = 0.6931471805599453
COUNT_ROWS = 8
PAIR = 2
STEPS = 4
TILE = 256
LANES = 128
FIRST_JOB = 2
LEAST = 2.0**-90
MOST = 2.0**120
VMEM_BYTES = 24 << 20
F32 = jnp.float32
BF16 = jnp.bfloat16


def dot(a, b, dims):
    return lax.dot_general(a, b, (dims, ((), ())), preferred_element_type=F32)


def thirds(x):
    parts = []
    for _ in range(3):
        parts.append(x.astype(BF16))
        x = x - parts[-1].astype(F32)
    return parts


def score_kernel(slots, caps, share, last, meta_ref, lanes_ref, q_ref, bank_ref, *refs):
    past, refs = (refs[:1], refs[1:]) if share else ((), refs)
    outs, refs = refs[: 1 + last], refs[1 + last :]
    out_ref, (rows_ref, soft_ref, bad_ref, a_ref, b_ref) = refs[0] if last else outs[0], refs[last:]
    blocks, rounds = q_ref.shape[:2]
    videos, tokens = bank_ref.shape[0] // 2, bank_ref.shape[1]
    total_rows = meta_ref[3, share]

    def pack(i, carry):
        r, g = i // blocks, i % blocks
        piece = q_ref[g, r].astype(F32)
        for c in range(caps):
            start = meta_ref[0, (share * rounds * blocks + i) * caps + c]
            rows_ref[pl.ds(start, slots), :] = piece[c * slots : (c + 1) * slots]
        return carry

    lax.fori_loop(0, rounds * blocks, pack, 0)
    lane = lax.broadcasted_iota(jnp.int32, (1, LANES), 1)
    here = lane // (rounds * blocks * caps) == share
    first = lanes_ref[0:1, :]
    end = jnp.where(here, first + lanes_ref[1:2, :], 0)
    scale = F32(SHARPNESS * LOG2E)
    jobs = [(0, FIRST_JOB), (FIRST_JOB, 2 * videos - FIRST_JOB)]
    bufs = (a_ref, b_ref)

    def products(dst, job, w):
        first, size = job
        bank = bank_ref[first : first + size].reshape(size * tokens, bank_ref.shape[2])
        dst[...] = dot(jnp.concatenate([bank, bank], axis=1), w, ((1,), (1,)))

    def unit(src, v, col, shifted):
        x = src[v * tokens : (v + 1) * tokens, col : col + LANES].reshape(tokens // 8, 8, LANES)
        if not shifted:
            return None, jnp.sum(jnp.sum(jnp.exp2(x), axis=0), axis=0, keepdims=True)
        top = jnp.max(x, axis=0)
        total = jnp.sum(jnp.exp2(x - top[None]), axis=0)
        peak = jnp.max(top, axis=0, keepdims=True)
        return peak, jnp.sum(total * jnp.exp2(top - peak), axis=0, keepdims=True)

    def weights(i):
        q = rows_ref[pl.ds(pl.multiple_of(i * TILE, TILE), TILE), :] * scale
        high = q.astype(BF16)
        return jnp.concatenate([high, (q - high.astype(F32)).astype(BF16)], axis=1)

    def collect(i, shifted):
        sums = soft_ref[1]
        soft = jnp.log2(sums)
        if shifted:
            soft = soft + soft_ref[0]
        col = i * TILE + lax.broadcasted_iota(jnp.int32, soft.shape, 1)
        valid = (col >= 0) & (col < total_rows)
        if not shifted:
            fine = (sums > LEAST) & (sums < MOST)
            bad_ref[...] = jnp.where(valid & ~fine, 1.0, bad_ref[...])
        soft = jnp.where(valid, soft * F32(LN2 / SHARPNESS), 0.0)
        parts = jnp.concatenate(thirds(soft), axis=0)
        row = i * TILE + lax.broadcasted_iota(jnp.int32, (TILE, LANES), 0)
        n = 2 * videos
        member = jnp.where((row >= first) & (row < end), F32(1), F32(0))
        got = dot(parts, member.astype(BF16), ((1,), (0,)))
        out_ref[...] += got[:n] + got[n : 2 * n] + got[2 * n :]

    def tile(shifted, i, carry):
        w = weights(i)
        collect(i - 1, shifted)
        for j, (base, size) in enumerate(jobs):
            after = (jobs[j + 1], w) if j + 1 < len(jobs) else (jobs[0], weights(i + 1))
            products(bufs[(j + 1) % 2], *after)
            for v in range(size):
                for col in range(0, TILE, LANES):
                    peak, total = unit(bufs[j % 2], v, col, shifted)
                    at = base + v
                    if shifted:
                        soft_ref[0, at : at + 1, col : col + LANES] = peak
                    soft_ref[1, at : at + 1, col : col + LANES] = total
        return carry

    tiles = (total_rows + TILE - 1) // TILE

    def run(shifted):
        out_ref[...] = past[0][...] if past else jnp.zeros_like(out_ref)
        products(bufs[0], jobs[0], weights(0))
        lax.fori_loop(0, tiles, functools.partial(tile, shifted), 0)
        collect(tiles - 1, shifted)

    bad_ref[...] = jnp.zeros_like(bad_ref)
    run(False)

    @pl.when(jnp.max(bad_ref[...]) > 0)
    def _():
        run(True)

    if last:
        mean = out_ref[...] / jnp.maximum(lanes_ref[1:2, :], 1).astype(F32)
        column = lax.broadcasted_iota(jnp.int32, (rounds * LANES, LANES), 0)
        spread = jnp.where(column == lanes_ref[2:3, :], F32(1), F32(0)).astype(BF16)
        n = 2 * videos
        got = dot(jnp.concatenate(thirds(mean), axis=0), spread, ((1,), (1,)))
        got = got[:n] + got[n : 2 * n] + got[2 * n :]
        outs[0][...] = got[:videos]
        outs[1][...] = got[videos:]


def share_scores(slots, caps, share, last, meta, query, bank, *past):
    blocks, rounds, rows, width = query.shape
    videos, tokens = bank.shape[0] // 2, bank.shape[1]
    n_rows = -(-(rounds * blocks * rows) // TILE) * TILE + TILE + slots
    vmem = pl.BlockSpec(memory_space=pltpu.VMEM)
    work = 2 * videos * tokens * rounds * blocks * rows
    total = (2 * videos, LANES)
    outs = [(videos, rounds * LANES)] * 2 if last else [total]
    return pl.pallas_call(
        lambda *refs: score_kernel(slots, caps, share, last, *refs),
        in_specs=[pl.BlockSpec(memory_space=pltpu.SMEM)] + [vmem] * (3 + len(past)),
        out_specs=[vmem] * len(outs),
        out_shape=[jax.ShapeDtypeStruct(shape, F32) for shape in outs],
        scratch_shapes=[pltpu.VMEM(total, F32)] * last
        + [
            pltpu.VMEM((n_rows, width), F32),
            pltpu.VMEM((2, 2 * videos, TILE), F32),
            pltpu.VMEM((2 * videos, TILE), F32),
            pltpu.VMEM((FIRST_JOB * tokens, TILE), F32),
            pltpu.VMEM(((2 * videos - FIRST_JOB) * tokens, TILE), F32),
        ],
        compiler_params=pltpu.CompilerParams(vmem_limit_bytes=VMEM_BYTES),
        cost_estimate=pl.CostEstimate(
            flops=4 * work * width, transcendentals=work, bytes_accessed=bank.size * 2
        ),
        name="soft_scores",
    )(meta, meta, query, bank, *past)


def merge_kernel(own_ref, tok_ref, pair_ref, both_ref, bank_ref, sems):
    videos, half = own_ref.shape[:2]
    moves = []
    for k, src in enumerate((own_ref, tok_ref, pair_ref, both_ref)):
        dst = bank_ref.at[pl.ds(k // 2 * videos, videos), pl.ds(k % 2 * half, half), :]
        moves.append(pltpu.make_async_copy(src, dst, sems.at[k]))
        moves[-1].start()
    for move in moves:
        move.wait()


def tables_kernel(caps, blocks, inner, quarters, vid_axis, tok_axis, counts_ref, meta_ref):
    rounds = counts_ref.shape[0]
    vid = lax.axis_index(vid_axis)
    quarter = vid % PAIR * (quarters // PAIR) + lax.axis_index(tok_axis)
    place = vid // PAIR % inner
    per = rounds * blocks * caps

    def where(lane):
        share, rest = lane // per, lane % per
        block = rest // caps % blocks * inner + (share ^ place)
        return share, rest // (blocks * caps), (block * quarters + quarter) * caps + lane % caps

    down = lax.broadcasted_iota(jnp.int32, (LANES, LANES), 0)
    across = lax.broadcasted_iota(jnp.int32, (LANES, LANES), 1)
    share, turn, cap = where(lax.broadcasted_iota(jnp.int32, (1, LANES), 1))
    used = share < inner
    counts = jnp.zeros((COUNT_ROWS, LANES), F32)
    for r in range(rounds):
        pick = jnp.where((down == cap) & (turn == r) & used, F32(1), F32(0)).astype(BF16)
        counts = counts + dot(counts_ref[r], pick, ((1,), (0,)))
    before = jnp.where((down < across) & (down // per == share), F32(1), F32(0)).astype(BF16)
    within = jnp.where(down // per == across, F32(1), F32(0)).astype(BF16)
    starts = dot(counts.astype(BF16), before, ((1,), (0,)))
    totals = dot(counts.astype(BF16), within, ((1,), (0,)))
    meta_ref[...] = jnp.zeros_like(meta_ref)
    meta_ref[0:1, :] = starts[:1].astype(jnp.int32)
    meta_ref[1:2, :] = counts[:1].astype(jnp.int32)
    meta_ref[2:3, :] = jnp.where(used, turn * LANES + cap, -1)
    meta_ref[3:4, :] = totals[:1].astype(jnp.int32)


def prepare_kernel(tok_axis, block_ref, counts_ref, out_ref, piece_ref, count_ref, in_sems, out_sems):
    n, rows = block_ref.shape[0], block_ref.shape[2]
    tok = lax.axis_index(tok_axis)
    lengths = pltpu.make_async_copy(counts_ref, count_ref, in_sems.at[2 * n])
    lengths.start()
    part = rows // 2
    parts = [(i, h) for i in range(n) for h in range(2)]
    moves = []
    for k, (i, h) in enumerate(parts):
        spot = pl.ds(h * part, part)
        moves.append(
            pltpu.make_async_copy(block_ref.at[i, tok, spot], piece_ref.at[i, spot], in_sems.at[k])
        )
        moves[-1].start()
    for k, (i, h) in enumerate(parts):
        moves[k].wait()
        spot = pl.ds(h * part, part)
        moves[k] = pltpu.make_async_copy(piece_ref.at[i, spot], out_ref.at[i, spot], out_sems.at[k])
        moves[k].start()
    lengths.wait()
    counts = jnp.broadcast_to(count_ref[...], (COUNT_ROWS, LANES)).astype(F32).astype(BF16)
    piece_ref[0, rows:, :] = counts
    for i in range(n):
        tail = piece_ref.at[0, pl.ds(rows, COUNT_ROWS)]
        spot = pl.ds(rows, COUNT_ROWS)
        moves.append(pltpu.make_async_copy(tail, out_ref.at[i, spot], out_sems.at[2 * n + i]))
        moves[-1].start()
    for move in moves:
        move.wait()


def pick_kernel(order_ref, shares_ref, wanted_ref, counts_ref):
    rows = shares_ref.shape[1] - COUNT_ROWS
    for r in range(order_ref.shape[0]):
        owner = order_ref[r]
        wanted_ref[r * rows : (r + 1) * rows, :] = shares_ref[owner, :rows, :]
        counts_ref[r] = shares_ref[owner, rows:, :]


def per_device(captions, caption_lengths, video_bank, owner_order):
    n_vid, n_tok = lax.axis_size("vid"), lax.axis_size("tok")
    capb, slots, width = captions.shape[1:]
    rounds = owner_order.shape[0]
    videos, half = video_bank.shape[:2]
    line = n_vid // PAIR
    caps = capb // (n_vid * n_tok)
    rows = caps * slots
    swap_tok = [(0, 1), (1, 0)]
    swap_pair = [(i, i ^ 1) for i in range(n_vid)]
    swap_both = [
        (i * n_tok + t, (i ^ 1) * n_tok + (t ^ 1)) for i in range(n_vid) for t in range(n_tok)
    ]
    vmem = pl.BlockSpec(memory_space=pltpu.VMEM)
    small = pltpu.CompilerParams(vmem_limit_bytes=VMEM_BYTES)

    tok_bank = lax.ppermute(video_bank, "tok", swap_tok)
    pair_bank = lax.ppermute(video_bank, "vid", swap_pair)
    both_bank = lax.ppermute(pair_bank, "tok", swap_tok)

    pieces = pl.pallas_call(
        lambda *refs: prepare_kernel("tok", *refs),
        in_specs=[pl.BlockSpec(memory_space=pltpu.HBM)] * 2,
        out_specs=pl.BlockSpec(memory_space=pltpu.HBM),
        out_shape=jax.ShapeDtypeStruct((n_vid, rows + COUNT_ROWS, width), captions.dtype),
        scratch_shapes=[
            pltpu.VMEM((n_vid, rows + COUNT_ROWS, width), captions.dtype),
            pltpu.VMEM(caption_lengths.shape, caption_lengths.dtype),
            pltpu.SemaphoreType.DMA((2 * n_vid + 1,)),
            pltpu.SemaphoreType.DMA((3 * n_vid,)),
        ],
        name="prepare",
    )(captions.reshape(n_vid, n_tok, rows, width), caption_lengths)
    shares = lax.all_to_all(pieces, "vid", 0, 0, tiled=True)
    bank = pl.pallas_call(
        merge_kernel,
        in_specs=[pl.BlockSpec(memory_space=pl.ANY)] * 4,
        out_specs=vmem,
        out_shape=jax.ShapeDtypeStruct((2 * videos, 2 * half, width), video_bank.dtype),
        scratch_shapes=[pltpu.SemaphoreType.DMA((4,))],
        compiler_params=small,
        name="merge",
    )(video_bank, tok_bank, pair_bank, both_bank)
    wanted, counts = pl.pallas_call(
        pick_kernel,
        in_specs=[pl.BlockSpec(memory_space=pltpu.SMEM), vmem],
        out_specs=[vmem] * 2,
        out_shape=[
            jax.ShapeDtypeStruct((rounds * rows, width), captions.dtype),
            jax.ShapeDtypeStruct((rounds, COUNT_ROWS, width), captions.dtype),
        ],
        compiler_params=small,
        name="pick",
    )(owner_order, shares)
    inner = min(STEPS, line)
    blocks = line // inner
    if blocks > 1:
        groups = [
            [(b * inner + m) * PAIR + s for b in range(blocks)] for m in range(inner) for s in range(PAIR)
        ]
        wanted = lax.all_gather(wanted, "vid", axis=0, axis_index_groups=groups)
    wanted = wanted.reshape(blocks, rounds, rows, width)
    arrived = [wanted]
    for k in range(1, inner):
        steps = [(i, i ^ (k * PAIR)) for i in range(n_vid)]
        arrived.append(lax.ppermute(wanted, "vid", steps))

    meta = pl.pallas_call(
        lambda *refs: tables_kernel(caps, blocks, inner, PAIR * n_tok, "vid", "tok", *refs),
        in_specs=[vmem],
        out_specs=vmem,
        out_shape=jax.ShapeDtypeStruct((8, LANES), jnp.int32),
        compiler_params=small,
        name="tables",
    )(counts)
    total = ()
    for k, query in enumerate(arrived):
        total = share_scores(slots, caps, k, k == inner - 1, meta, query, bank, *total)
    near, far = total
    near = near + lax.ppermute(near, "tok", swap_tok)
    return near + lax.ppermute(far, "vid", swap_pair) + lax.ppermute(far, ("vid", "tok"), swap_both)


def solution(mesh):
    return jax.shard_map(
        per_device,
        mesh=mesh,
        in_specs=(
            P(("groups", "vid"), None, None, None),
            P(("groups", "vid"), None),
            P(("groups", "vid"), "tok", None),
            P("groups"),
        ),
        out_specs=P(("groups", "vid"), None),
        check_vma=False,
    )
```

```python
import functools

import jax
import jax.numpy as jnp
from jax import lax
from jax.experimental import pallas as pl
from jax.experimental.pallas import tpu as pltpu
from jax.sharding import PartitionSpec as P


SHARPNESS = 5.0
LOG2E = 1.4426950408889634
LN2 = 0.6931471805599453
COUNT_ROWS = 8
PAIR = 2
STEPS = 4
TILE = 256
LANES = 128
FIRST_JOB = 2
LEAST = 2.0**-90
MOST = 2.0**120
VMEM_BYTES = 24 << 20
F32 = jnp.float32
BF16 = jnp.bfloat16


def dot(a, b, dims):
    return lax.dot_general(a, b, (dims, ((), ())), preferred_element_type=F32)


def thirds(x):
    parts = []
    for _ in range(3):
        parts.append(x.astype(BF16))
        x = x - parts[-1].astype(F32)
    return parts


def score_kernel(slots, caps, share, last, meta_ref, lanes_ref, q_ref, bank_ref, *refs):
    past, refs = (refs[:1], refs[1:]) if share else ((), refs)
    outs, refs = refs[: 1 + last], refs[1 + last :]
    out_ref, (rows_ref, soft_ref, bad_ref, a_ref, b_ref) = refs[0] if last else outs[0], refs[last:]
    blocks, rounds = q_ref.shape[:2]
    videos, tokens = bank_ref.shape[0] // 2, bank_ref.shape[1]
    total_rows = meta_ref[3, share]

    def pack(i, carry):
        r, g = i // blocks, i % blocks
        piece = q_ref[g, r].astype(F32)
        for c in range(caps):
            start = meta_ref[0, (share * rounds * blocks + i) * caps + c]
            rows_ref[pl.ds(start, slots), :] = piece[c * slots : (c + 1) * slots]
        return carry

    lax.fori_loop(0, rounds * blocks, pack, 0)
    lane = lax.broadcasted_iota(jnp.int32, (1, LANES), 1)
    here = lane // (rounds * blocks * caps) == share
    first = lanes_ref[0:1, :]
    end = jnp.where(here, first + lanes_ref[1:2, :], 0)
    scale = F32(SHARPNESS * LOG2E)
    jobs = [(0, FIRST_JOB), (FIRST_JOB, 2 * videos - FIRST_JOB)]
    bufs = (a_ref, b_ref)

    def products(dst, job, w):
        first, size = job
        bank = bank_ref[first : first + size].reshape(size * tokens, bank_ref.shape[2])
        dst[...] = dot(jnp.concatenate([bank, bank], axis=1), w, ((1,), (1,)))

    def unit(src, v, col, shifted):
        x = src[v * tokens : (v + 1) * tokens, col : col + LANES].reshape(tokens // 8, 8, LANES)
        if not shifted:
            return None, jnp.sum(jnp.sum(jnp.exp2(x), axis=0), axis=0, keepdims=True)
        top = jnp.max(x, axis=0)
        total = jnp.sum(jnp.exp2(x - top[None]), axis=0)
        peak = jnp.max(top, axis=0, keepdims=True)
        return peak, jnp.sum(total * jnp.exp2(top - peak), axis=0, keepdims=True)

    def weights(i):
        q = rows_ref[pl.ds(pl.multiple_of(i * TILE, TILE), TILE), :] * scale
        high = q.astype(BF16)
        return jnp.concatenate([high, (q - high.astype(F32)).astype(BF16)], axis=1)

    def collect(i, shifted):
        sums = soft_ref[1]
        soft = jnp.log2(sums)
        if shifted:
            soft = soft + soft_ref[0]
        col = i * TILE + lax.broadcasted_iota(jnp.int32, soft.shape, 1)
        valid = (col >= 0) & (col < total_rows)
        if not shifted:
            fine = (sums > LEAST) & (sums < MOST)
            bad_ref[...] = jnp.where(valid & ~fine, 1.0, bad_ref[...])
        soft = jnp.where(valid, soft * F32(LN2 / SHARPNESS), 0.0)
        parts = jnp.concatenate(thirds(soft), axis=0)
        row = i * TILE + lax.broadcasted_iota(jnp.int32, (TILE, LANES), 0)
        n = 2 * videos
        member = jnp.where((row >= first) & (row < end), F32(1), F32(0))
        got = dot(parts, member.astype(BF16), ((1,), (0,)))
        out_ref[...] += got[:n] + got[n : 2 * n] + got[2 * n :]

    def tile(shifted, i, carry):
        w = weights(i)
        collect(i - 1, shifted)
        for j, (base, size) in enumerate(jobs):
            after = (jobs[j + 1], w) if j + 1 < len(jobs) else (jobs[0], weights(i + 1))
            products(bufs[(j + 1) % 2], *after)
            for v in range(size):
                for col in range(0, TILE, LANES):
                    peak, total = unit(bufs[j % 2], v, col, shifted)
                    at = base + v
                    if shifted:
                        soft_ref[0, at : at + 1, col : col + LANES] = peak
                    soft_ref[1, at : at + 1, col : col + LANES] = total
        return carry

    tiles = (total_rows + TILE - 1) // TILE

    def run(shifted):
        out_ref[...] = past[0][...] if past else jnp.zeros_like(out_ref)
        products(bufs[0], jobs[0], weights(0))
        lax.fori_loop(0, tiles, functools.partial(tile, shifted), 0)
        collect(tiles - 1, shifted)

    bad_ref[...] = jnp.zeros_like(bad_ref)
    run(False)

    @pl.when(jnp.max(bad_ref[...]) > 0)
    def _():
        run(True)

    if last:
        mean = out_ref[...] / jnp.maximum(lanes_ref[1:2, :], 1).astype(F32)
        column = lax.broadcasted_iota(jnp.int32, (rounds * LANES, LANES), 0)
        spread = jnp.where(column == lanes_ref[2:3, :], F32(1), F32(0)).astype(BF16)
        n = 2 * videos
        got = dot(jnp.concatenate(thirds(mean), axis=0), spread, ((1,), (1,)))
        got = got[:n] + got[n : 2 * n] + got[2 * n :]
        outs[0][...] = got[:videos]
        outs[1][...] = got[videos:]


def share_scores(slots, caps, share, last, meta, query, bank, *past):
    blocks, rounds, rows, width = query.shape
    videos, tokens = bank.shape[0] // 2, bank.shape[1]
    n_rows = -(-(rounds * blocks * rows) // TILE) * TILE + TILE + slots
    vmem = pl.BlockSpec(memory_space=pltpu.VMEM)
    work = 2 * videos * tokens * rounds * blocks * rows
    total = (2 * videos, LANES)
    outs = [(videos, rounds * LANES)] * 2 if last else [total]
    return pl.pallas_call(
        lambda *refs: score_kernel(slots, caps, share, last, *refs),
        in_specs=[pl.BlockSpec(memory_space=pltpu.SMEM)] + [vmem] * (3 + len(past)),
        out_specs=[vmem] * len(outs),
        out_shape=[jax.ShapeDtypeStruct(shape, F32) for shape in outs],
        scratch_shapes=[pltpu.VMEM(total, F32)] * last
        + [
            pltpu.VMEM((n_rows, width), F32),
            pltpu.VMEM((2, 2 * videos, TILE), F32),
            pltpu.VMEM((2 * videos, TILE), F32),
            pltpu.VMEM((FIRST_JOB * tokens, TILE), F32),
            pltpu.VMEM(((2 * videos - FIRST_JOB) * tokens, TILE), F32),
        ],
        compiler_params=pltpu.CompilerParams(vmem_limit_bytes=VMEM_BYTES),
        cost_estimate=pl.CostEstimate(
            flops=4 * work * width, transcendentals=work, bytes_accessed=bank.size * 2
        ),
        name="soft_scores",
    )(meta, meta, query, bank, *past)


def merge_kernel(caps, blocks, inner, quarters, vid_axis, tok_axis, order_ref, own_ref, tok_ref,
                 pair_ref, both_ref, shares_ref, bank_ref, meta_ref, sems):
    videos, half = own_ref.shape[:2]
    rounds = order_ref.shape[0]
    moves = []
    for k, src in enumerate((own_ref, tok_ref, pair_ref, both_ref)):
        dst = bank_ref.at[pl.ds(k // 2 * videos, videos), pl.ds(k % 2 * half, half), :]
        moves.append(pltpu.make_async_copy(src, dst, sems.at[k]))
        moves[-1].start()
    vid = lax.axis_index(vid_axis)
    quarter = vid % PAIR * (quarters // PAIR) + lax.axis_index(tok_axis)
    place = vid // PAIR % inner
    per = rounds * blocks * caps

    def where(lane):
        share, rest = lane // per, lane % per
        block = rest // caps % blocks * inner + (share ^ place)
        return share, rest // (blocks * caps), (block * quarters + quarter) * caps + lane % caps

    down = lax.broadcasted_iota(jnp.int32, (LANES, LANES), 0)
    across = lax.broadcasted_iota(jnp.int32, (LANES, LANES), 1)
    share, turn, cap = where(lax.broadcasted_iota(jnp.int32, (1, LANES), 1))
    used = share < inner
    counts = jnp.zeros((COUNT_ROWS, LANES), F32)
    for r in range(rounds):
        pick = jnp.where((down == cap) & (turn == r) & used, F32(1), F32(0)).astype(BF16)
        lengths = shares_ref[order_ref[r], shares_ref.shape[1] - COUNT_ROWS :, :]
        counts = counts + dot(lengths, pick, ((1,), (0,)))
    before = jnp.where((down < across) & (down // per == share), F32(1), F32(0)).astype(BF16)
    within = jnp.where(down // per == across, F32(1), F32(0)).astype(BF16)
    starts = dot(counts.astype(BF16), before, ((1,), (0,)))
    totals = dot(counts.astype(BF16), within, ((1,), (0,)))
    meta_ref[...] = jnp.zeros_like(meta_ref)
    meta_ref[0:1, :] = starts[:1].astype(jnp.int32)
    meta_ref[1:2, :] = counts[:1].astype(jnp.int32)
    meta_ref[2:3, :] = jnp.where(used, turn * LANES + cap, -1)
    meta_ref[3:4, :] = totals[:1].astype(jnp.int32)
    for move in moves:
        move.wait()


def prepare_kernel(tok_axis, block_ref, counts_ref, out_ref, piece_ref, count_ref, in_sems, out_sems):
    n, rows = block_ref.shape[0], block_ref.shape[2]
    tok = lax.axis_index(tok_axis)
    lengths = pltpu.make_async_copy(counts_ref, count_ref, in_sems.at[n])
    lengths.start()
    moves = []
    for k in range(n):
        moves.append(
            pltpu.make_async_copy(block_ref.at[k, tok], piece_ref.at[k, pl.ds(0, rows)], in_sems.at[k])
        )
        moves[-1].start()
    lengths.wait()
    counts = jnp.broadcast_to(count_ref[...], (COUNT_ROWS, LANES)).astype(F32).astype(BF16)
    for k in range(n):
        piece_ref[k, rows:, :] = counts
    for k in range(n):
        moves[k].wait()
        moves[k] = pltpu.make_async_copy(piece_ref.at[k], out_ref.at[k], out_sems.at[k])
        moves[k].start()
    for move in moves:
        move.wait()


def per_device(captions, caption_lengths, video_bank, owner_order):
    n_vid, n_tok = lax.axis_size("vid"), lax.axis_size("tok")
    capb, slots, width = captions.shape[1:]
    rounds = owner_order.shape[0]
    videos, half = video_bank.shape[:2]
    line = n_vid // PAIR
    caps = capb // (n_vid * n_tok)
    rows = caps * slots
    swap_tok = [(0, 1), (1, 0)]
    swap_pair = [(i, i ^ 1) for i in range(n_vid)]
    swap_both = [
        (i * n_tok + t, (i ^ 1) * n_tok + (t ^ 1)) for i in range(n_vid) for t in range(n_tok)
    ]
    vmem = pl.BlockSpec(memory_space=pltpu.VMEM)
    small = pltpu.CompilerParams(vmem_limit_bytes=VMEM_BYTES)

    tok_bank = lax.ppermute(video_bank, "tok", swap_tok)
    pair_bank = lax.ppermute(video_bank, "vid", swap_pair)

    pieces = pl.pallas_call(
        lambda *refs: prepare_kernel("tok", *refs),
        in_specs=[pl.BlockSpec(memory_space=pltpu.HBM)] * 2,
        out_specs=pl.BlockSpec(memory_space=pltpu.HBM),
        out_shape=jax.ShapeDtypeStruct((n_vid, rows + COUNT_ROWS, width), captions.dtype),
        scratch_shapes=[
            pltpu.VMEM((n_vid, rows + COUNT_ROWS, width), captions.dtype),
            pltpu.VMEM(caption_lengths.shape, caption_lengths.dtype),
            pltpu.SemaphoreType.DMA((n_vid + 1,)),
            pltpu.SemaphoreType.DMA((n_vid,)),
        ],
        name="prepare",
    )(captions.reshape(n_vid, n_tok, rows, width), caption_lengths)
    shares = lax.all_to_all(pieces, "vid", 0, 0, tiled=True)
    wanted = jnp.concatenate(
        [lax.dynamic_index_in_dim(shares, owner_order[r], 0, keepdims=False)[:rows] for r in range(rounds)]
    )
    inner = min(STEPS, line)
    blocks = line // inner
    if blocks > 1:
        groups = [
            [(b * inner + m) * PAIR + s for b in range(blocks)] for m in range(inner) for s in range(PAIR)
        ]
        wanted = lax.all_gather(wanted, "vid", axis=0, axis_index_groups=groups)
    wanted = wanted.reshape(blocks, rounds, rows, width)
    arrived = [wanted]
    for k in range(1, inner):
        steps = [(i, i ^ (k * PAIR)) for i in range(n_vid)]
        arrived.append(lax.ppermute(wanted, "vid", steps))

    both_bank = lax.ppermute(pair_bank, "tok", swap_tok)
    bank, meta = pl.pallas_call(
        lambda *refs: merge_kernel(caps, blocks, inner, PAIR * n_tok, "vid", "tok", *refs),
        in_specs=[pl.BlockSpec(memory_space=pltpu.SMEM)]
        + [pl.BlockSpec(memory_space=pl.ANY)] * 4
        + [vmem],
        out_specs=[vmem] * 2,
        out_shape=[
            jax.ShapeDtypeStruct((2 * videos, 2 * half, width), video_bank.dtype),
            jax.ShapeDtypeStruct((8, LANES), jnp.int32),
        ],
        scratch_shapes=[pltpu.SemaphoreType.DMA((4,))],
        compiler_params=small,
        name="merge",
    )(owner_order, video_bank, tok_bank, pair_bank, both_bank, shares)
    total = ()
    for k, query in enumerate(arrived):
        total = share_scores(slots, caps, k, k == inner - 1, meta, query, bank, *total)
    near, far = total
    near = near + lax.ppermute(near, "tok", swap_tok)
    return near + lax.ppermute(far, "vid", swap_pair) + lax.ppermute(far, ("vid", "tok"), swap_both)


def solution(mesh):
    return jax.shard_map(
        per_device,
        mesh=mesh,
        in_specs=(
            P(("groups", "vid"), None, None, None),
            P(("groups", "vid"), None),
            P(("groups", "vid"), "tok", None),
            P("groups"),
        ),
        out_specs=P(("groups", "vid"), None),
        check_vma=False,
    )
```

```python
import functools

import jax
import jax.numpy as jnp
from jax import lax
from jax.experimental import pallas as pl
from jax.experimental.pallas import tpu as pltpu
from jax.sharding import PartitionSpec as P


SHARPNESS = 5.0
LOG2E = 1.4426950408889634
LN2 = 0.6931471805599453
COUNT_ROWS = 8
PAIR = 2
STEPS = 4
TILE = 256
LANES = 128
FIRST_JOB = 2
LEAST = 2.0**-90
MOST = 2.0**120
VMEM_BYTES = 24 << 20
F32 = jnp.float32
BF16 = jnp.bfloat16


def dot(a, b, dims):
    return lax.dot_general(a, b, (dims, ((), ())), preferred_element_type=F32)


def thirds(x):
    parts = []
    for _ in range(3):
        parts.append(x.astype(BF16))
        x = x - parts[-1].astype(F32)
    return parts


def score_kernel(slots, caps, share, last, meta_ref, lanes_ref, q_ref, bank_ref, *refs):
    past, refs = (refs[:1], refs[1:]) if share else ((), refs)
    outs, refs = refs[: 1 + last], refs[1 + last :]
    out_ref, (rows_ref, soft_ref, bad_ref, a_ref, b_ref, w_ref) = refs[0] if last else outs[0], refs[last:]
    blocks, rounds = q_ref.shape[:2]
    videos, tokens = bank_ref.shape[0] // 2, bank_ref.shape[1]
    total_rows = meta_ref[3, share]

    def pack(i, carry):
        r, g = i // blocks, i % blocks
        piece = q_ref[g, r].astype(F32)
        for c in range(caps):
            start = meta_ref[0, (share * rounds * blocks + i) * caps + c]
            rows_ref[pl.ds(start, slots), :] = piece[c * slots : (c + 1) * slots]
        return carry

    lax.fori_loop(0, rounds * blocks, pack, 0)
    lane = lax.broadcasted_iota(jnp.int32, (1, LANES), 1)
    here = lane // (rounds * blocks * caps) == share
    first = lanes_ref[0:1, :]
    end = jnp.where(here, first + lanes_ref[1:2, :], 0)
    scale = F32(SHARPNESS * LOG2E)
    jobs = [(0, FIRST_JOB), (FIRST_JOB, 2 * videos - FIRST_JOB)]
    bufs = (a_ref, b_ref)

    def products(dst, job, w):
        first, size = job
        bank = bank_ref[first : first + size].reshape(size * tokens, bank_ref.shape[2])
        dst[...] = dot(jnp.concatenate([bank, bank], axis=1), w, ((1,), (1,)))

    def unit(src, v, col, shifted):
        x = src[v * tokens : (v + 1) * tokens, col : col + LANES].reshape(tokens // 8, 8, LANES)
        if not shifted:
            return None, jnp.sum(jnp.sum(jnp.exp2(x), axis=0), axis=0, keepdims=True)
        top = jnp.max(x, axis=0)
        total = jnp.sum(jnp.exp2(x - top[None]), axis=0)
        peak = jnp.max(top, axis=0, keepdims=True)
        return peak, jnp.sum(total * jnp.exp2(top - peak), axis=0, keepdims=True)

    def weights(i):
        q = rows_ref[pl.ds(pl.multiple_of(i * TILE, TILE), TILE), :] * scale
        high = q.astype(BF16)
        return jnp.concatenate([high, (q - high.astype(F32)).astype(BF16)], axis=1)

    def collect(i, shifted):
        sums = soft_ref[1]
        soft = jnp.log2(sums)
        if shifted:
            soft = soft + soft_ref[0]
        col = i * TILE + lax.broadcasted_iota(jnp.int32, soft.shape, 1)
        valid = (col >= 0) & (col < total_rows)
        if not shifted:
            fine = (sums > LEAST) & (sums < MOST)
            bad_ref[...] = jnp.where(valid & ~fine, 1.0, bad_ref[...])
        soft = jnp.where(valid, soft * F32(LN2 / SHARPNESS), 0.0)
        parts = jnp.concatenate(thirds(soft), axis=0)
        row = i * TILE + lax.broadcasted_iota(jnp.int32, (TILE, LANES), 0)
        n = 2 * videos
        member = jnp.where((row >= first) & (row < end), F32(1), F32(0))
        got = dot(parts, member.astype(BF16), ((1,), (0,)))
        out_ref[...] += got[:n] + got[n : 2 * n] + got[2 * n :]

    def tile(shifted, i, carry):
        w = w_ref[...]
        collect(i - 1, shifted)
        for j, (base, size) in enumerate(jobs):
            if j + 1 < len(jobs):
                after = (jobs[j + 1], w)
            else:
                nxt = weights(i + 1)
                w_ref[...] = nxt
                after = (jobs[0], nxt)
            products(bufs[(j + 1) % 2], *after)
            for v in range(size):
                for col in range(0, TILE, LANES):
                    peak, total = unit(bufs[j % 2], v, col, shifted)
                    at = base + v
                    if shifted:
                        soft_ref[0, at : at + 1, col : col + LANES] = peak
                    soft_ref[1, at : at + 1, col : col + LANES] = total
        return carry

    tiles = (total_rows + TILE - 1) // TILE

    def run(shifted):
        out_ref[...] = past[0][...] if past else jnp.zeros_like(out_ref)
        w0 = weights(0)
        w_ref[...] = w0
        products(bufs[0], jobs[0], w0)
        lax.fori_loop(0, tiles, functools.partial(tile, shifted), 0)
        collect(tiles - 1, shifted)

    bad_ref[...] = jnp.zeros_like(bad_ref)
    run(False)

    @pl.when(jnp.max(bad_ref[...]) > 0)
    def _():
        run(True)

    if last:
        mean = out_ref[...] / jnp.maximum(lanes_ref[1:2, :], 1).astype(F32)
        column = lax.broadcasted_iota(jnp.int32, (rounds * LANES, LANES), 0)
        spread = jnp.where(column == lanes_ref[2:3, :], F32(1), F32(0)).astype(BF16)
        n = 2 * videos
        got = dot(jnp.concatenate(thirds(mean), axis=0), spread, ((1,), (1,)))
        got = got[:n] + got[n : 2 * n] + got[2 * n :]
        outs[0][...] = got[:videos]
        outs[1][...] = got[videos:]


def share_scores(slots, caps, share, last, meta, query, bank, *past):
    blocks, rounds, rows, width = query.shape
    videos, tokens = bank.shape[0] // 2, bank.shape[1]
    n_rows = -(-(rounds * blocks * rows) // TILE) * TILE + TILE + slots
    vmem = pl.BlockSpec(memory_space=pltpu.VMEM)
    work = 2 * videos * tokens * rounds * blocks * rows
    total = (2 * videos, LANES)
    outs = [(videos, rounds * LANES)] * 2 if last else [total]
    return pl.pallas_call(
        lambda *refs: score_kernel(slots, caps, share, last, *refs),
        in_specs=[pl.BlockSpec(memory_space=pltpu.SMEM)] + [vmem] * (3 + len(past)),
        out_specs=[vmem] * len(outs),
        out_shape=[jax.ShapeDtypeStruct(shape, F32) for shape in outs],
        scratch_shapes=[pltpu.VMEM(total, F32)] * last
        + [
            pltpu.VMEM((n_rows, width), F32),
            pltpu.VMEM((2, 2 * videos, TILE), F32),
            pltpu.VMEM((2 * videos, TILE), F32),
            pltpu.VMEM((FIRST_JOB * tokens, TILE), F32),
            pltpu.VMEM(((2 * videos - FIRST_JOB) * tokens, TILE), F32),
            pltpu.VMEM((TILE, 2 * width), BF16),
        ],
        compiler_params=pltpu.CompilerParams(vmem_limit_bytes=VMEM_BYTES),
        cost_estimate=pl.CostEstimate(
            flops=4 * work * width, transcendentals=work, bytes_accessed=bank.size * 2
        ),
        name="soft_scores",
    )(meta, meta, query, bank, *past)


def merge_kernel(caps, blocks, inner, quarters, vid_axis, tok_axis, order_ref, own_ref, tok_ref,
                 pair_ref, both_ref, shares_ref, bank_ref, meta_ref, sems):
    videos, half = own_ref.shape[:2]
    rounds = order_ref.shape[0]
    moves = []
    for k, src in enumerate((own_ref, tok_ref, pair_ref, both_ref)):
        dst = bank_ref.at[pl.ds(k // 2 * videos, videos), pl.ds(k % 2 * half, half), :]
        moves.append(pltpu.make_async_copy(src, dst, sems.at[k]))
        moves[-1].start()
    vid = lax.axis_index(vid_axis)
    quarter = vid % PAIR * (quarters // PAIR) + lax.axis_index(tok_axis)
    place = vid // PAIR % inner
    per = rounds * blocks * caps

    def where(lane):
        share, rest = lane // per, lane % per
        block = rest // caps % blocks * inner + (share ^ place)
        return share, rest // (blocks * caps), (block * quarters + quarter) * caps + lane % caps

    down = lax.broadcasted_iota(jnp.int32, (LANES, LANES), 0)
    across = lax.broadcasted_iota(jnp.int32, (LANES, LANES), 1)
    share, turn, cap = where(lax.broadcasted_iota(jnp.int32, (1, LANES), 1))
    used = share < inner
    counts = jnp.zeros((COUNT_ROWS, LANES), F32)
    for r in range(rounds):
        pick = jnp.where((down == cap) & (turn == r) & used, F32(1), F32(0)).astype(BF16)
        lengths = shares_ref[order_ref[r], shares_ref.shape[1] - COUNT_ROWS :, :]
        counts = counts + dot(lengths, pick, ((1,), (0,)))
    before = jnp.where((down < across) & (down // per == share), F32(1), F32(0)).astype(BF16)
    within = jnp.where(down // per == across, F32(1), F32(0)).astype(BF16)
    starts = dot(counts.astype(BF16), before, ((1,), (0,)))
    totals = dot(counts.astype(BF16), within, ((1,), (0,)))
    meta_ref[...] = jnp.zeros_like(meta_ref)
    meta_ref[0:1, :] = starts[:1].astype(jnp.int32)
    meta_ref[1:2, :] = counts[:1].astype(jnp.int32)
    meta_ref[2:3, :] = jnp.where(used, turn * LANES + cap, -1)
    meta_ref[3:4, :] = totals[:1].astype(jnp.int32)
    for move in moves:
        move.wait()


def prepare_kernel(tok_axis, block_ref, counts_ref, out_ref, piece_ref, count_ref, in_sems, out_sems):
    n, rows = block_ref.shape[0], block_ref.shape[2]
    tok = lax.axis_index(tok_axis)
    lengths = pltpu.make_async_copy(counts_ref, count_ref, in_sems.at[n])
    lengths.start()
    moves = []
    for k in range(n):
        moves.append(
            pltpu.make_async_copy(block_ref.at[k, tok], piece_ref.at[k, pl.ds(0, rows)], in_sems.at[k])
        )
        moves[-1].start()
    lengths.wait()
    counts = jnp.broadcast_to(count_ref[...], (COUNT_ROWS, LANES)).astype(F32).astype(BF16)
    for k in range(n):
        piece_ref[k, rows:, :] = counts
    for k in range(n):
        moves[k].wait()
        moves[k] = pltpu.make_async_copy(piece_ref.at[k], out_ref.at[k], out_sems.at[k])
        moves[k].start()
    for move in moves:
        move.wait()


def per_device(captions, caption_lengths, video_bank, owner_order):
    n_vid, n_tok = lax.axis_size("vid"), lax.axis_size("tok")
    capb, slots, width = captions.shape[1:]
    rounds = owner_order.shape[0]
    videos, half = video_bank.shape[:2]
    line = n_vid // PAIR
    caps = capb // (n_vid * n_tok)
    rows = caps * slots
    swap_tok = [(0, 1), (1, 0)]
    swap_pair = [(i, i ^ 1) for i in range(n_vid)]
    swap_both = [
        (i * n_tok + t, (i ^ 1) * n_tok + (t ^ 1)) for i in range(n_vid) for t in range(n_tok)
    ]
    vmem = pl.BlockSpec(memory_space=pltpu.VMEM)
    small = pltpu.CompilerParams(vmem_limit_bytes=VMEM_BYTES)

    tok_bank = lax.ppermute(video_bank, "tok", swap_tok)
    pair_bank = lax.ppermute(video_bank, "vid", swap_pair)

    pieces = pl.pallas_call(
        lambda *refs: prepare_kernel("tok", *refs),
        in_specs=[pl.BlockSpec(memory_space=pltpu.HBM)] * 2,
        out_specs=pl.BlockSpec(memory_space=pltpu.HBM),
        out_shape=jax.ShapeDtypeStruct((n_vid, rows + COUNT_ROWS, width), captions.dtype),
        scratch_shapes=[
            pltpu.VMEM((n_vid, rows + COUNT_ROWS, width), captions.dtype),
            pltpu.VMEM(caption_lengths.shape, caption_lengths.dtype),
            pltpu.SemaphoreType.DMA((n_vid + 1,)),
            pltpu.SemaphoreType.DMA((n_vid,)),
        ],
        name="prepare",
    )(captions.reshape(n_vid, n_tok, rows, width), caption_lengths)
    shares = lax.all_to_all(pieces, "vid", 0, 0, tiled=True)
    wanted = jnp.concatenate(
        [lax.dynamic_index_in_dim(shares, owner_order[r], 0, keepdims=False)[:rows] for r in range(rounds)]
    )
    inner = min(STEPS, line)
    blocks = line // inner
    if blocks > 1:
        groups = [
            [(b * inner + m) * PAIR + s for b in range(blocks)] for m in range(inner) for s in range(PAIR)
        ]
        wanted = lax.all_gather(wanted, "vid", axis=0, axis_index_groups=groups)
    wanted = wanted.reshape(blocks, rounds, rows, width)
    arrived = [wanted]
    for k in range(1, inner):
        steps = [(i, i ^ (k * PAIR)) for i in range(n_vid)]
        arrived.append(lax.ppermute(wanted, "vid", steps))

    both_bank = lax.ppermute(pair_bank, "tok", swap_tok)
    bank, meta = pl.pallas_call(
        lambda *refs: merge_kernel(caps, blocks, inner, PAIR * n_tok, "vid", "tok", *refs),
        in_specs=[pl.BlockSpec(memory_space=pltpu.SMEM)]
        + [pl.BlockSpec(memory_space=pl.ANY)] * 4
        + [vmem],
        out_specs=[vmem] * 2,
        out_shape=[
            jax.ShapeDtypeStruct((2 * videos, 2 * half, width), video_bank.dtype),
            jax.ShapeDtypeStruct((8, LANES), jnp.int32),
        ],
        scratch_shapes=[pltpu.SemaphoreType.DMA((4,))],
        compiler_params=small,
        name="merge",
    )(owner_order, video_bank, tok_bank, pair_bank, both_bank, shares)
    total = ()
    for k, query in enumerate(arrived):
        total = share_scores(slots, caps, k, k == inner - 1, meta, query, bank, *total)
    near, far = total
    near = near + lax.ppermute(near, "tok", swap_tok)
    return near + lax.ppermute(far, "vid", swap_pair) + lax.ppermute(far, ("vid", "tok"), swap_both)


def solution(mesh):
    return jax.shard_map(
        per_device,
        mesh=mesh,
        in_specs=(
            P(("groups", "vid"), None, None, None),
            P(("groups", "vid"), None),
            P(("groups", "vid"), "tok", None),
            P("groups"),
        ),
        out_specs=P(("groups", "vid"), None),
        check_vma=False,
    )
```
